1024 devices in a mesh: section: 64 (over z, x), ctx: 16 (over y, core).
Axes of the slice: x: 4, y: 8, z: 16, core: 2. Of those that a mesh axis runs over, the one named last changes fastest.
Arguments:
- activations: bfloat16 [64, 24, 8192], P('section'), may hold values from -6 to 6
- act_frames: int32 [64, 24], replicated, may hold values from 0 to 191
- fresh_batch: bfloat16 [24, 8192], replicated, may hold values from -6 to 6
- fresh_frames: int32 [24], replicated, may hold values from 0 to 191
- norm_gain: float32 [64, 8192], P('section'), may hold values from 0.1 to 1.9
- cached_keys: bfloat16 [64, 12288, 1024], P('section', 'ctx'), may hold values from -64 to 64
- cached_values: bfloat16 [64, 12288, 1024], P('section', 'ctx'), may hold values from -6 to 6
- key_frames: int32 [12288], P('ctx'), may hold values from 0 to 191, never falling along the last dimension, each value on 1 to 128 neighbouring positions
Outputs:
- result: bfloat16 [64, 24, 8192], P('section')
The draws below stay inside these ranges and needn't reach their ends.
Inputs may be any that keep to these rules, and one draw needn't show every extreme that they name: `key_frames`: frame indices never fall along the clip, and every frame of 0 to 191 holds at least one token.
All inputs are finite; a program needn't handle non-finite values.
Results may differ from the reference program's by a relative error of at most 0.019.
Values may be sent and summed in bfloat16 or wider, within the bound.
A program may use at most 64 MiB of HBM per device.

```python
import math
import jax
import jax.numpy as jnp
import numpy as np
from jax import lax

HEADS = 64
KVH = 8
HD = 128
D = 8192
Q_TOK = 24
CTX_DEV = 768
SECTIONS = 64
CTXTOK = 12288
FRAMES = 192
N_CTX = 16


def draw_cached_keys(key, part):
    key_one = jax.random.fold_in(key, 0)
    full_shape = (SECTIONS, CTXTOK, KVH * HD)
    return jnp.clip(jax.random.normal(key_one, full_shape, jnp.float32), -6.0, 6.0).astype(jnp.bfloat16)


def set_ends(entries, own_key, smallest, top_value):
    index_at = [jax.random.randint(jax.random.fold_in(own_key, axis), (), 0, length) for axis, length in enumerate(entries.shape)]
    widest = entries.shape.index(max(entries.shape))
    beside = index_at[:widest] + [(index_at[widest] + 1) % entries.shape[widest]] + index_at[widest + 1:]
    return entries.at[tuple(index_at)].set(smallest).at[tuple(beside)].set(top_value)


def steps_of(key, dims, pieces, least, largest):
    level, own = 1.0, jax.random.fold_in(key, 6)
    for dim, parts in pieces:
        heights = jnp.exp(jax.random.uniform(jax.random.fold_in(own, dim), (parts,), jnp.float32, least / len(pieces), largest / len(pieces)))
        level = level * jnp.repeat(heights, dims[dim] // parts).reshape([-1 if axis == dim else 1 for axis in range(len(dims))])
    return level


def split_up(count, total, most, lean):
    loads = [(1 << 20) // math.isqrt(rank ** lean) + 1 for rank in range(2, count + 1)]
    surplus, holding = total - most - (count - 1), [1] * (count - 1)
    while surplus > 0:
        movable = [i for i in range(count - 1) if holding[i] < most]
        whole, left = sum([loads[i] for i in movable]), surplus
        for i in movable:
            addition = min(most - holding[i], max(1, left * loads[i] // whole), surplus)
            holding[i] = holding[i] + addition
            surplus = surplus - addition
    return np.array([most] + holding)


def ragged_sizes(stream_key, count, total, reach, skew):
    if count == 2:
        one = jax.random.randint(stream_key, (), max(1, total - reach), min(reach, total - 1) + 1)
        return jnp.stack([one, total - one])
    sizes = jnp.asarray(split_up(count, total, reach, skew), jnp.int32)
    twos = (count - 1) // 2
    donor, sink = sizes[1:1 + 2 * twos:2], sizes[2:2 + 2 * twos:2]
    margin = jnp.minimum(donor - 1, reach - sink)
    passed = jax.random.randint(jax.random.fold_in(stream_key, 1), (twos,), 0, 1 << 20) % (margin + 1)
    sizes = sizes.at[1:1 + 2 * twos:2].set(donor - passed).at[2:2 + 2 * twos:2].set(sink + passed)
    return sizes[jax.random.permutation(jax.random.fold_in(stream_key, 2), count)]


def bell_draw(own_key, extent, width, reach, cuts=(), kind=jnp.bfloat16):
    factor_of = steps_of(own_key, extent, cuts, -0.22, 0.18) if cuts else 1.0
    array = jax.random.normal(own_key, extent, jnp.float32) * width * factor_of
    return jnp.minimum(jnp.maximum(array, -reach), reach).astype(kind)


def setup_inputs(seed: int = 0) -> dict:
    arg_keys = jax.random.split(jax.random.key(seed), 9)
    return {
        "activations": bell_draw(arg_keys[0], (SECTIONS, Q_TOK, D), 1.0, 6.0, ((0, 64),)),
        "act_frames": set_ends(jax.random.randint(arg_keys[1], (SECTIONS, Q_TOK), 0, FRAMES), jax.random.fold_in(arg_keys[1], 1), 0, FRAMES - 1).astype(jnp.int32),
        "fresh_batch": bell_draw(arg_keys[2], (Q_TOK, D), 1.0, 6.0),
        "fresh_frames": set_ends(jax.random.randint(arg_keys[3], (Q_TOK,), 0, FRAMES), jax.random.fold_in(arg_keys[3], 1), 0, FRAMES - 1).astype(jnp.int32),
        "norm_gain": jnp.clip(1.0 + 0.18 * jax.random.normal(arg_keys[4], (SECTIONS, D), jnp.float32), 0.1, 1.9),
        "cached_keys": draw_cached_keys(jax.random.fold_in(arg_keys[8], 71), 0),
        "cached_values": bell_draw(arg_keys[6], (SECTIONS, CTXTOK, KVH * HD), 1.0, 6.0, ((0, 64), (1, 16))),
        "key_frames": jnp.searchsorted(jnp.cumsum(ragged_sizes(arg_keys[7], FRAMES, CTXTOK, min(128, CTXTOK), 0)), jnp.arange(CTXTOK), side="right").astype(jnp.int32),
    }


epsilon = 1e-05
masked_score = -1e+30

def block_terms(grouped, frames, key_block, value_block, frame_block):
    scores = jnp.einsum('tkgd,jkd->tkgj', grouped.astype(jnp.float32), key_block.astype(jnp.float32)) * HD ** (-0.5)
    visible = frame_block[None, None, None, :] <= frames[:, None, None, None]
    scores = jnp.where(visible, scores, masked_score)
    block_max = lax.optimization_barrier(jnp.max(scores, axis=-1))
    probabilities = jnp.where(visible, jnp.exp(scores - block_max[..., None]), 0.0).astype(jnp.bfloat16)
    totals = lax.optimization_barrier(jnp.sum(probabilities.astype(jnp.float32), axis=-1))
    weighted = jnp.einsum('tkgj,jkd->tkgd', probabilities.astype(jnp.float32), value_block.astype(jnp.float32))
    return (block_max, totals, weighted)

def layer(hidden, frames, norm_scale, key_cache, value_cache, key_frames):
    widened = hidden.astype(jnp.float32)
    per_head = widened.reshape(Q_TOK, HEADS, HD)
    scale_heads = norm_scale.reshape(HEADS, HD)
    queries = (per_head * lax.rsqrt(lax.optimization_barrier(jnp.mean(per_head * per_head, axis=-1, keepdims=True)) + epsilon) * scale_heads[None]).astype(jnp.bfloat16)
    grouped = queries.reshape(Q_TOK, KVH, HEADS // KVH, HD)
    key_blocks = key_cache.reshape(N_CTX, CTX_DEV, KVH, HD)
    value_blocks = value_cache.reshape(N_CTX, CTX_DEV, KVH, HD)
    frame_blocks = key_frames.reshape(N_CTX, CTX_DEV)

    def one_block(blocks):
        return block_terms(grouped, frames, blocks[0], blocks[1], blocks[2])
    maxima, totals, weighted = lax.map(one_block, (key_blocks, value_blocks, frame_blocks))
    overall = lax.optimization_barrier(jnp.max(maxima, axis=0))
    factors = jnp.exp(maxima - overall[None])
    numerator = lax.optimization_barrier(jnp.sum(factors[..., None] * weighted, axis=0))
    denominator = lax.optimization_barrier(jnp.sum(factors * totals, axis=0))
    attended = (numerator / denominator[..., None]).reshape(Q_TOK, HEADS * HD)
    return (widened + attended).astype(jnp.bfloat16)

def reference(activations, act_frames, fresh_batch, fresh_frames, norm_gain, cached_keys, cached_values, key_frames):

    def first_tick(section_index):
        return layer(activations[section_index], act_frames[section_index], norm_gain[section_index], cached_keys[section_index], cached_values[section_index], key_frames)
    handed = lax.map(first_tick, jnp.arange(SECTIONS, dtype=jnp.int32))
    incoming = jnp.concatenate([fresh_batch[None], handed[:-1]], axis=0)
    frames_in = jnp.concatenate([fresh_frames[None], act_frames[:-1]], axis=0)

    def second_tick(section_index):
        return layer(incoming[section_index], frames_in[section_index], norm_gain[section_index], cached_keys[section_index], cached_values[section_index], key_frames)
    return lax.map(second_tick, jnp.arange(SECTIONS, dtype=jnp.int32))
```

```python
import functools
import math

import jax
import jax.numpy as jnp
from jax import lax
from jax.experimental import pallas as pl
from jax.experimental.pallas import tpu as pltpu
from jax.sharding import PartitionSpec as P

HD = 128
GROUP = 8
EPSILON = 1e-05
MASKED = -1e30
MESH = pl.DeviceIdType.MESH
EXPONENT_SCALE = HD**-0.5 * math.log2(math.e)


def kernel(
    n_sections,
    n_chips,
    act_hbm,
    act_frames_hbm,
    fresh_hbm,
    fresh_frames_hbm,
    gain_hbm,
    keys_hbm,
    values_hbm,
    key_frames_hbm,
    out_ref,
    act,
    fresh,
    act_frames,
    fresh_frames,
    gain,
    key_frames,
    keys,
    values,
    bias,
    scores,
    probs,
    sent,
    sent_stats,
    arrived,
    arrived_stats,
    combined,
    handed,
    local_sem,
    keys_sem,
    values_sem,
    pair_send_sem,
    pair_recv_sem,
    frames_send_sem,
    frames_recv_sem,
    part_send_sem,
    part_recv_sem,
    stat_send_sem,
    stat_recv_sem,
    hand_send_sem,
    hand_recv_sem,
    out_send_sem,
    out_recv_sem,
    cross_send_sem,
    cross_recv_sem,
):
    tokens = act.shape[0]
    own_keys = keys_hbm.shape[0]
    kv_heads = keys.shape[0]
    plane = act.shape[1]
    chunk_columns = plane // n_chips
    heads_in_chunk = chunk_columns // HD
    chunk_rows = heads_in_chunk * tokens
    chunks_per_head = GROUP * tokens // chunk_rows

    section = lax.axis_index("section")
    ctx = lax.axis_index("ctx")
    chip, core = ctx // 2, ctx % 2
    other = 1 - core
    following = (section + 1) % n_sections
    previous = (section + n_sections - 1) % n_sections
    sibling = (section, chip * 2 + other)

    def in_section(j):
        return (section, j * 2 + core)

    def columns(j, width):
        return pl.ds(pl.multiple_of(j * width, width), width)

    own_rows = pl.ds(pl.multiple_of(core * own_keys, own_keys), own_keys)
    locals_ = [
        pltpu.make_async_copy(act_hbm.at[:, columns(core, plane)], act, local_sem.at[0]),
        pltpu.make_async_copy(act_frames_hbm, act_frames, local_sem.at[1]),
        pltpu.make_async_copy(fresh_hbm.at[:, columns(core, plane)], fresh, local_sem.at[2]),
        pltpu.make_async_copy(fresh_frames_hbm, fresh_frames, local_sem.at[3]),
        pltpu.make_async_copy(gain_hbm.at[:, columns(core, plane)], gain, local_sem.at[4]),
        pltpu.make_async_copy(key_frames_hbm, key_frames.at[core], local_sem.at[5]),
    ]
    for copy in locals_:
        copy.start()

    def own_copies(h):
        return (
            pltpu.make_async_copy(
                keys_hbm.at[:, columns(core * kv_heads + h, HD)],
                keys.at[h, own_rows, :],
                keys_sem.at[h],
            ),
            pltpu.make_async_copy(
                values_hbm.at[:, columns(core * kv_heads + h, HD)],
                values.at[h, own_rows, pl.ds(0, HD)],
                values_sem.at[h],
            ),
        )

    def pair_copies(h):
        return (
            pltpu.make_async_remote_copy(
                src_ref=keys_hbm.at[:, columns(other * kv_heads + h, HD)],
                dst_ref=keys.at[h, own_rows, :],
                send_sem=pair_send_sem.at[h, 0],
                recv_sem=pair_recv_sem.at[h, 0],
                device_id=sibling,
                device_id_type=MESH,
            ),
            pltpu.make_async_remote_copy(
                src_ref=values_hbm.at[:, columns(other * kv_heads + h, HD)],
                dst_ref=values.at[h, own_rows, pl.ds(0, HD)],
                send_sem=pair_send_sem.at[h, 1],
                recv_sem=pair_recv_sem.at[h, 1],
                device_id=sibling,
                device_id_type=MESH,
            ),
        )

    other_rows = pl.ds(pl.multiple_of(other * own_keys, own_keys), own_keys)

    def pair_arrivals(h):
        return (
            pltpu.make_async_remote_copy(
                src_ref=keys.at[h, other_rows, :],
                dst_ref=keys.at[h, other_rows, :],
                send_sem=pair_send_sem.at[h, 0],
                recv_sem=pair_recv_sem.at[h, 0],
                device_id=sibling,
                device_id_type=MESH,
            ),
            pltpu.make_async_remote_copy(
                src_ref=values.at[h, other_rows, pl.ds(0, HD)],
                dst_ref=values.at[h, other_rows, pl.ds(0, HD)],
                send_sem=pair_send_sem.at[h, 1],
                recv_sem=pair_recv_sem.at[h, 1],
                device_id=sibling,
                device_id_type=MESH,
            ),
        )

    def visit(i):
        step = jnp.where(i == 0, 2, jnp.where(i == 1, 1, jnp.where(i == 2, 3, 0)))
        return (chip // chunks_per_head + step) % kv_heads

    for i in range(kv_heads):
        for copy in own_copies(visit(i)):
            copy.start()

    barrier = pltpu.get_barrier_semaphore()
    pl.semaphore_signal(barrier, inc=1, device_id=sibling, device_id_type=MESH)

    @pl.loop(0, n_chips)
    def _(j):
        @pl.when(j != chip)
        def _():
            pl.semaphore_signal(barrier, inc=1, device_id=in_section(j), device_id_type=MESH)

        for side in (previous, following):
            pl.semaphore_signal(
                barrier, inc=1, device_id=(side, j * 2 + core), device_id_type=MESH
            )

    pl.semaphore_wait(barrier, 1 + (n_chips - 1) + 2 * n_chips)

    frames_copy = pltpu.make_async_remote_copy(
        src_ref=key_frames_hbm,
        dst_ref=key_frames.at[core],
        send_sem=frames_send_sem,
        recv_sem=frames_recv_sem,
        device_id=sibling,
        device_id_type=MESH,
    )
    frames_copy.start()
    for i in range(kv_heads):
        for copy in pair_copies(visit(i)):
            copy.start()

    for h in range(kv_heads):
        values[h, :, HD:] = jnp.ones((values.shape[1], HD), values.dtype)
    for copy in locals_:
        copy.wait()
    frames_copy.wait()

    def set_bias(row):
        rows = lax.broadcasted_iota(jnp.int32, (tokens, tokens), 0)
        lanes = lax.broadcasted_iota(jnp.int32, (tokens, tokens), 1)
        spread = jnp.broadcast_to(row, (tokens, tokens)).astype(jnp.float32)
        column = jnp.sum(jnp.where(rows == lanes, spread, 0.0), axis=1, keepdims=True)
        for side in range(2):
            frames = key_frames[side].astype(jnp.float32)
            shown = jnp.where(frames <= column, 0.0, MASKED)
            bias[0:tokens, side * own_keys : (side + 1) * own_keys] = shown
            bias[tokens : 2 * tokens, side * own_keys : (side + 1) * own_keys] = shown

    def part_copy(tick, j):
        return pltpu.make_async_remote_copy(
            src_ref=sent.at[tick, j],
            dst_ref=arrived.at[tick, chip],
            send_sem=part_send_sem.at[tick, j],
            recv_sem=part_recv_sem.at[tick, chip],
            device_id=in_section(j),
            device_id_type=MESH,
        )

    def stat_copy(tick, j):
        return pltpu.make_async_remote_copy(
            src_ref=sent_stats.at[tick, j],
            dst_ref=arrived_stats.at[tick, chip],
            send_sem=stat_send_sem.at[tick, j],
            recv_sem=stat_recv_sem.at[tick, chip],
            device_id=in_section(j),
            device_id_type=MESH,
        )

    def part_arrival(tick, j):
        return pltpu.make_async_remote_copy(
            src_ref=sent.at[tick, j],
            dst_ref=arrived.at[tick, j],
            send_sem=part_send_sem.at[tick, j],
            recv_sem=part_recv_sem.at[tick, j],
            device_id=in_section(j),
            device_id_type=MESH,
        )

    def stat_arrival(tick, j):
        return pltpu.make_async_remote_copy(
            src_ref=sent_stats.at[tick, j],
            dst_ref=arrived_stats.at[tick, j],
            send_sem=stat_send_sem.at[tick, j],
            recv_sem=stat_recv_sem.at[tick, j],
            device_id=in_section(j),
            device_id_type=MESH,
        )

    def attend(tick, h, hidden):
        head_gain = gain[:, columns(h, GROUP * HD)]
        rows = []
        for g in range(GROUP):
            x = hidden[:, g * HD : (g + 1) * HD]
            mean = jnp.mean(x * x, axis=1, keepdims=True)
            rows.append(x * lax.rsqrt(mean + EPSILON) * head_gain[:, g * HD : (g + 1) * HD])
        queries = jnp.concatenate(rows, axis=0).astype(jnp.bfloat16)
        scores[...] = lax.dot_general(
            queries, keys[h], (((1,), (1,)), ((), ())), preferred_element_type=jnp.float32
        )
        block = 2 * tokens
        maxima = []
        for g in range(GROUP * tokens // block):
            part = scores[g * block : (g + 1) * block, :] + bias[...]
            top = jnp.max(part, axis=1, keepdims=True)
            maxima.append(top)
            probs[g * block : (g + 1) * block, :] = jnp.exp2(
                (part - top) * EXPONENT_SCALE
            ).astype(jnp.bfloat16)
        top = jnp.concatenate(maxima, axis=0)
        product = lax.dot_general(
            probs[...], values[h], (((1,), (0,)), ((), ())), preferred_element_type=jnp.float32
        )
        lanes = lax.broadcasted_iota(jnp.int32, (chunk_rows, HD), 1)
        for q in range(chunks_per_head):
            j = h * chunks_per_head + q
            span = slice(q * chunk_rows, (q + 1) * chunk_rows)
            weighted = product[span, :HD].astype(jnp.bfloat16)
            stats = jnp.where(lanes == 0, top[span], product[span, HD:])
            stats = jnp.concatenate(
                [stats, jnp.ones((HD - chunk_rows, HD), jnp.float32)], axis=0
            )
            stats = stats.T[0:8]

            @pl.when(j == chip)
            def _(weighted=weighted, stats=stats):
                arrived[tick, chip] = weighted
                arrived_stats[tick, chip] = stats

            @pl.when(j != chip)
            def _(j=j, weighted=weighted, stats=stats):
                sent[tick, j] = weighted
                sent_stats[tick, j] = stats
                part_copy(tick, j).start()
                stat_copy(tick, j).start()

    def combine(tick, residual):
        @pl.loop(0, n_chips)
        def _(j):
            @pl.when(j != chip)
            def _():
                part_arrival(tick, j).wait()
                stat_arrival(tick, j).wait()

        tops = arrived_stats[tick, :, 0, :]
        totals = arrived_stats[tick, :, 1, :]
        overall = jnp.max(tops, axis=0, keepdims=True)
        factors = jnp.exp2((tops - overall) * EXPONENT_SCALE)
        factors = factors / jnp.sum(factors * totals, axis=0, keepdims=True)
        factors = jnp.concatenate(
            [factors, jnp.zeros((HD - n_chips, HD), jnp.float32)], axis=0
        ).T
        attended = jnp.zeros((chunk_rows, HD), jnp.float32)
        for j in range(n_chips):
            attended += factors[:chunk_rows, j : j + 1] * arrived[tick, j].astype(jnp.float32)
        for g in range(heads_in_chunk):
            lanes = slice(g * HD, (g + 1) * HD)
            combined[tick, :, lanes] = (
                residual[:, lanes] + attended[g * tokens : (g + 1) * tokens]
            ).astype(jnp.bfloat16)

    set_bias(act_frames[pl.ds(section, 1), :])

    @pl.loop(0, kv_heads)
    def _(i):
        h = visit(i)
        for copy in own_copies(h):
            copy.wait()
        for copy in pair_arrivals(h):
            copy.wait_recv()
        for copy in pair_copies(h):
            copy.wait_send()
        attend(0, h, act[:, columns(h, GROUP * HD)].astype(jnp.float32))

    combine(0, act[:, columns(chip, chunk_columns)].astype(jnp.float32))

    def hand_copy(j):
        return pltpu.make_async_remote_copy(
            src_ref=combined.at[0],
            dst_ref=handed.at[:, columns(chip, chunk_columns)],
            send_sem=hand_send_sem.at[j],
            recv_sem=hand_recv_sem.at[chip],
            device_id=(following, j * 2 + core),
            device_id_type=MESH,
        )

    def hand_arrival(j):
        return pltpu.make_async_remote_copy(
            src_ref=combined.at[0],
            dst_ref=handed.at[:, columns(j, chunk_columns)],
            send_sem=hand_send_sem.at[j],
            recv_sem=hand_recv_sem.at[j],
            device_id=(previous, j * 2 + core),
            device_id_type=MESH,
        )

    @pl.loop(0, n_chips)
    def _(k):
        hand_copy((chip + n_chips // 2 + k) % n_chips).start()

    first = section == 0
    set_bias(jnp.where(first, fresh_frames[...], act_frames[pl.ds(previous, 1), :]))

    def incoming(span):
        return jnp.where(
            first, fresh[:, span].astype(jnp.float32), handed[:, span].astype(jnp.float32)
        )

    @pl.loop(0, kv_heads)
    def _(i):
        h = visit(i)
        for q in range(chunks_per_head):
            hand_arrival(h * chunks_per_head + q).wait_recv()
        attend(1, h, incoming(columns(h, GROUP * HD)))

    combine(1, incoming(columns(chip, chunk_columns)))

    def result_columns(half, j):
        return pl.ds(pl.multiple_of(half * plane + j * chunk_columns, chunk_columns), chunk_columns)

    def out_copy(j):
        return pltpu.make_async_remote_copy(
            src_ref=combined.at[1],
            dst_ref=out_ref.at[:, result_columns(core, chip)],
            send_sem=out_send_sem.at[j],
            recv_sem=out_recv_sem.at[chip],
            device_id=in_section(j),
            device_id_type=MESH,
        )

    def out_arrival(j):
        return pltpu.make_async_remote_copy(
            src_ref=combined.at[1],
            dst_ref=out_ref.at[:, result_columns(core, j)],
            send_sem=out_send_sem.at[j],
            recv_sem=out_recv_sem.at[j],
            device_id=in_section(j),
            device_id_type=MESH,
        )

    def cross_copy(j, half):
        return pltpu.make_async_remote_copy(
            src_ref=out_ref.at[:, result_columns(half, j)],
            dst_ref=out_ref.at[:, result_columns(half, j)],
            send_sem=cross_send_sem.at[j],
            recv_sem=cross_recv_sem.at[j],
            device_id=sibling,
            device_id_type=MESH,
        )

    @pl.loop(0, n_chips)
    def _(k):
        j = (chip + n_chips // 2 + k) % n_chips

        @pl.when(j != chip)
        def _():
            out_copy(j).start()

    out_ref[:, result_columns(core, chip)] = combined[1]
    cross_copy(chip, core).start()

    @pl.loop(1, n_chips)
    def _(k):
        away = (k + 1) // 2
        j = (chip + jnp.where(k % 2 == 1, away, n_chips - away)) % n_chips
        out_arrival(j).wait_recv()
        cross_copy(j, core).start()

    @pl.loop(0, n_chips)
    def _(j):
        cross_copy(j, other).wait_recv()
        cross_copy(j, core).wait_send()
        hand_copy(j).wait_send()

        @pl.when(j != chip)
        def _():
            out_copy(j).wait_send()


def attention(n_sections, n_chips, act, act_frames, fresh, fresh_frames, gain, keys, values, key_frames):
    tokens, width = act.shape
    own_keys = keys.shape[0]
    plane = width // 2
    kv_heads = plane // (GROUP * HD)
    chunk_columns = plane // n_chips
    chunk_rows = chunk_columns // HD * tokens
    dma = pltpu.SemaphoreType.DMA
    anywhere = pl.BlockSpec(memory_space=pl.ANY)
    return pl.pallas_call(
        functools.partial(kernel, n_sections, n_chips),
        out_shape=jax.ShapeDtypeStruct((tokens, width), jnp.bfloat16),
        in_specs=[anywhere] * 8,
        out_specs=pl.BlockSpec(memory_space=pltpu.VMEM),
        scratch_shapes=[
            pltpu.VMEM((tokens, plane), jnp.bfloat16),
            pltpu.VMEM((tokens, plane), jnp.bfloat16),
            pltpu.VMEM(act_frames.shape, jnp.int32),
            pltpu.VMEM(fresh_frames.shape, jnp.int32),
            pltpu.VMEM((1, plane), jnp.float32),
            pltpu.VMEM((2, 1, own_keys), jnp.int32),
            pltpu.VMEM((kv_heads, 2 * own_keys, HD), jnp.bfloat16),
            pltpu.VMEM((kv_heads, 2 * own_keys, 2 * HD), jnp.bfloat16),
            pltpu.VMEM((2 * tokens, 2 * own_keys), jnp.float32),
            pltpu.VMEM((GROUP * tokens, 2 * own_keys), jnp.float32),
            pltpu.VMEM((GROUP * tokens, 2 * own_keys), jnp.bfloat16),
            pltpu.VMEM((2, n_chips, chunk_rows, HD), jnp.bfloat16),
            pltpu.VMEM((2, n_chips, 8, HD), jnp.float32),
            pltpu.VMEM((2, n_chips, chunk_rows, HD), jnp.bfloat16),
            pltpu.VMEM((2, n_chips, 8, HD), jnp.float32),
            pltpu.VMEM((2, tokens, chunk_columns), jnp.bfloat16),
            pltpu.VMEM((tokens, plane), jnp.bfloat16),
            dma((6,)),
            dma((kv_heads,)),
            dma((kv_heads,)),
            dma((kv_heads, 2)),
            dma((kv_heads, 2)),
            dma,
            dma,
            dma((2, n_chips)),
            dma((2, n_chips)),
            dma((2, n_chips)),
            dma((2, n_chips)),
            dma((n_chips,)),
            dma((n_chips,)),
            dma((n_chips,)),
            dma((n_chips,)),
            dma((n_chips,)),
            dma((n_chips,)),
        ],
        compiler_params=pltpu.CompilerParams(
            collective_id=0, has_side_effects=True, vmem_limit_bytes=40 * 2**20
        ),
        name="two_ticks",
    )(act, act_frames, fresh, fresh_frames, gain, keys, values, key_frames)


def solution(mesh):
    n_sections, n_chips = mesh.shape["section"], mesh.shape["ctx"] // 2

    def body(act, act_frames, fresh, fresh_frames, gain, keys, values, key_frames):
        result = attention(
            n_sections,
            n_chips,
            act[0],
            act_frames,
            fresh,
            fresh_frames[None],
            gain,
            keys[0],
            values[0],
            key_frames[None],
        )
        return result[None]

    placed = (
        P("section", None, None),
        P(),
        P(),
        P(),
        P("section", None),
        P("section", "ctx", None),
        P("section", "ctx", None),
        P("ctx"),
    )
    return jax.shard_map(
        body, mesh=mesh, in_specs=placed, out_specs=P("section", None, None), check_vma=False
    )
```

```python
import functools
import math

import jax
import jax.numpy as jnp
from jax import lax
from jax.experimental import pallas as pl
from jax.experimental.pallas import tpu as pltpu
from jax.sharding import PartitionSpec as P

HD = 128
GROUP = 8
EPSILON = 1e-05
MASKED = -1e30
MESH = pl.DeviceIdType.MESH
EXPONENT_SCALE = HD**-0.5 * math.log2(math.e)
STAT_ROWS = 16


def frames_stride(count):
    return -(-count // 1024) * 1024


def remote(src, dst, send_sem, recv_sem, device):
    return pltpu.make_async_remote_copy(
        src_ref=src,
        dst_ref=dst,
        send_sem=send_sem,
        recv_sem=recv_sem,
        device_id=device,
        device_id_type=MESH,
    )


def kernel(
    n_sections,
    n_chips,
    act_hbm,
    act_frames_hbm,
    fresh_hbm,
    fresh_frames_hbm,
    gain_hbm,
    keys_hbm,
    values_hbm,
    key_frames_hbm,
    out_ref,
    act,
    fresh,
    act_frames,
    fresh_frames,
    gain,
    key_frames,
    keys,
    values,
    bias,
    parts,
    pair_arrived,
    sent,
    arrived,
    combined,
    handed,
    local_sem,
    keys_sem,
    values_sem,
    pair_send_sem,
    pair_recv_sem,
    cache_send_sem,
    cache_recv_sem,
    frames_send_sem,
    frames_recv_sem,
    part_send_sem,
    part_recv_sem,
    hand_send_sem,
    hand_recv_sem,
    out_send_sem,
    out_recv_sem,
    cross_send_sem,
    cross_recv_sem,
    line_sem,
):
    tokens = act.shape[0]
    own_keys = keys_hbm.shape[0]
    plane = fresh.shape[1]
    kv_heads = plane // (GROUP * HD)
    head_rows = GROUP * tokens
    chunk_columns = plane // n_chips
    heads_in_chunk = chunk_columns // HD
    chunk_rows = heads_in_chunk * tokens
    chunks_per_head = head_rows // chunk_rows

    section = lax.axis_index("section")
    ctx = lax.axis_index("ctx")
    chip, core = ctx // 2, ctx % 2
    other = 1 - core
    sibling = (section, chip * 2 + other)
    not_first = section != 0
    not_last = section != n_sections - 1

    def in_line(j):
        return (section, j * 2 + core)

    def columns(j, width):
        return pl.ds(pl.multiple_of(j * width, width), width)

    def far_first(k):
        half = n_chips // 2
        step = jnp.where(k % 2 == 1, half - (k + 1) // 2, half + k // 2)
        return (chip + step) % n_chips

    def slot_of(i, h):
        return jnp.where(i < kv_heads, 2 * kv_heads + h, 2 * h + core)

    def visit(i):
        i = i % kv_heads
        step = jnp.where(i == 0, 2, jnp.where(i == 1, 1, jnp.where(i == 2, 3, 0)))
        return (chip // chunks_per_head + step) % kv_heads

    def loads(i):
        h = visit(i)
        half = jnp.where(i < kv_heads, other, core)
        span = columns(half * kv_heads + h, HD)
        slot = slot_of(i, h)
        return (
            pltpu.make_async_copy(keys_hbm.at[:, span], keys.at[slot], keys_sem.at[i]),
            pltpu.make_async_copy(
                values_hbm.at[:, span], values.at[slot, :, pl.ds(0, HD)], values_sem.at[i]
            ),
        )

    stride = frames_stride(own_keys)
    own_frames = pl.ds(pl.multiple_of(core * stride, stride), own_keys)
    small = [
        pltpu.make_async_copy(act_hbm, act, local_sem.at[0]),
        pltpu.make_async_copy(act_frames_hbm, act_frames, local_sem.at[1]),
        pltpu.make_async_copy(gain_hbm, gain, local_sem.at[2]),
        pltpu.make_async_copy(key_frames_hbm, key_frames.at[own_frames], local_sem.at[3]),
    ]
    late = [
        pltpu.make_async_copy(fresh_hbm.at[:, columns(core, plane)], fresh, local_sem.at[4]),
        pltpu.make_async_copy(fresh_frames_hbm, fresh_frames, local_sem.at[5]),
    ]
    for copy in small:
        copy.start()

    barrier = pltpu.get_barrier_semaphore()
    pl.semaphore_signal(barrier, inc=1, device_id=sibling, device_id_type=MESH)

    @pl.loop(0, n_chips - 1)
    def _(k):
        pl.semaphore_signal(barrier, inc=1, device_id=in_line(far_first(k)), device_id_type=MESH)

    @pl.when(not_first)
    def _():
        pl.semaphore_signal(barrier, inc=1, device_id=(section - 1, ctx), device_id_type=MESH)

    @pl.when(not_last)
    def _():
        pl.semaphore_signal(barrier, inc=1, device_id=(section + 1, ctx), device_id_type=MESH)

    for i in range(2 * kv_heads):
        for copy in loads(i):
            copy.start()
    for copy in late:
        copy.start()
    for slot in range(values.shape[0]):
        values[slot, :, HD:] = jnp.ones((own_keys, HD), values.dtype)
    for copy in small:
        copy.wait()

    def held_frames(s):
        lanes = lax.broadcasted_iota(jnp.int32, act_frames.shape, 1)
        spread = act_frames[...].astype(jnp.float32)
        return jnp.sum(jnp.where(lanes == s, spread, 0.0), axis=1, keepdims=True)

    def entering_frames():
        rows = lax.broadcasted_iota(jnp.int32, (tokens, tokens), 0)
        lanes = lax.broadcasted_iota(jnp.int32, (tokens, tokens), 1)
        spread = jnp.broadcast_to(fresh_frames[...], (tokens, tokens)).astype(jnp.float32)
        return jnp.sum(jnp.where(rows == lanes, spread, 0.0), axis=1, keepdims=True)

    def shown(frames, column):
        row = key_frames[frames].astype(jnp.float32)[None]
        return jnp.where(row <= column, 0.0, MASKED)

    def queries_of(hidden, head_gain):
        rows = []
        for g in range(GROUP):
            span = slice(g * HD, (g + 1) * HD)
            x = hidden[:, span]
            mean = jnp.mean(x * x, axis=1, keepdims=True)
            rows.append(x * lax.rsqrt(mean + EPSILON) * head_gain[:, span])
        return jnp.concatenate(rows, axis=0).astype(jnp.bfloat16)

    def attend(queries, head_keys, head_values, mask):
        scores = lax.dot_general(
            queries, head_keys, (((1,), (1,)), ((), ())), preferred_element_type=jnp.float32
        )
        block = 2 * tokens
        maxima, probs = [], []
        for g in range(head_rows // block):
            part = scores[g * block : (g + 1) * block] + mask
            top = jnp.max(part, axis=1, keepdims=True)
            maxima.append(top)
            probs.append(jnp.exp2((part - top) * EXPONENT_SCALE).astype(jnp.bfloat16))
        product = lax.dot_general(
            jnp.concatenate(probs, axis=0),
            head_values,
            (((1,), (0,)), ((), ())),
            preferred_element_type=jnp.float32,
        )
        return jnp.concatenate(maxima, axis=0), product

    def part_copy(tick, j):
        return remote(
            sent.at[tick, j],
            arrived.at[tick, chip],
            part_send_sem.at[tick, j],
            part_recv_sem.at[tick, chip],
            in_line(j),
        )

    def part_arrival(tick, j):
        return remote(
            sent.at[tick, j],
            arrived.at[tick, j],
            part_send_sem.at[tick, j],
            part_recv_sem.at[tick, j],
            in_line(j),
        )

    def ship(tick, h, top, totals, weighted):
        lanes = lax.broadcasted_iota(jnp.int32, (chunk_rows, HD), 1)
        for q in range(chunks_per_head):
            j = h * chunks_per_head + q
            span = slice(q * chunk_rows, (q + 1) * chunk_rows)
            stats = jnp.where(lanes % 2 == 0, top[span], totals[span])
            high = stats.astype(jnp.bfloat16).astype(jnp.float32)
            middle = (stats - high).astype(jnp.bfloat16).astype(jnp.float32)
            low = stats - high - middle
            terms = jnp.where(lanes < 2, high, jnp.where(lanes < 4, middle, low))
            terms = jnp.concatenate(
                [terms, jnp.ones((HD - chunk_rows, HD), jnp.float32)], axis=0
            ).T[:STAT_ROWS]
            packet = jnp.concatenate([weighted[span], terms], axis=0).astype(jnp.bfloat16)

            @pl.when(j == chip)
            def _(packet=packet):
                arrived[tick, chip] = packet

            @pl.when(j != chip)
            def _(j=j, packet=packet):
                sent[tick, j] = packet
                part_copy(tick, j).start()

    def combine(tick, residual):
        @pl.loop(0, n_chips)
        def _(j):
            @pl.when(j != chip)
            def _():
                part_arrival(tick, j).wait()

        stats = arrived[tick, :, chunk_rows:, :].astype(jnp.float32)
        tops = stats[:, 0] + stats[:, 2] + stats[:, 4]
        totals = stats[:, 1] + stats[:, 3] + stats[:, 5]
        overall = jnp.max(tops, axis=0, keepdims=True)
        factors = jnp.exp2((tops - overall) * EXPONENT_SCALE)
        factors = factors / jnp.sum(factors * totals, axis=0, keepdims=True)
        factors = jnp.concatenate(
            [factors, jnp.zeros((HD - n_chips, HD), jnp.float32)], axis=0
        ).T
        attended = jnp.zeros((chunk_rows, HD), jnp.float32)
        for j in range(n_chips):
            weighted = arrived[tick, j, :chunk_rows].astype(jnp.float32)
            attended += factors[:chunk_rows, j : j + 1] * weighted
        for g in range(heads_in_chunk):
            lanes = slice(g * HD, (g + 1) * HD)
            combined[tick, :, lanes] = (
                residual[:, lanes] + attended[g * tokens : (g + 1) * tokens]
            ).astype(jnp.bfloat16)

    mask = shown(own_frames, held_frames(section))
    bias[0:tokens, 0:own_keys] = mask
    bias[tokens : 2 * tokens, 0:own_keys] = mask
    pair_lanes = lax.broadcasted_iota(jnp.int32, (head_rows, HD), 1)

    def first_tick(i):
        h = visit(i)
        half = jnp.where(i < kv_heads, other, core)
        span = columns(half * kv_heads + h, GROUP * HD)
        for copy in loads(i):
            copy.wait()
        slot = slot_of(i, h)
        queries = queries_of(act[:, span].astype(jnp.float32), gain[:, span])
        top, product = attend(queries, keys[slot], values[slot], bias[:, 0:own_keys])
        place = jnp.where(i < kv_heads, h, kv_heads + h)
        parts[place, :, :HD] = product[:, :HD]
        parts[place, :, HD:] = jnp.where(pair_lanes < HD // 2, top, product[:, HD:])

    @pl.loop(0, 2 * kv_heads - 2)
    def _(i):
        first_tick(i)

    pl.semaphore_wait(barrier, n_chips + not_first.astype(jnp.int32) + not_last.astype(jnp.int32))

    def pair_copy(h):
        return remote(
            parts.at[h], pair_arrived.at[h], pair_send_sem.at[h], pair_recv_sem.at[h], sibling
        )

    @pl.loop(0, kv_heads)
    def _(i):
        pair_copy(visit(i)).start()

    frames_copy = remote(
        key_frames_hbm, key_frames.at[own_frames], frames_send_sem, frames_recv_sem, sibling
    )
    frames_copy.start()

    @pl.when(not_first)
    def _():
        pl.semaphore_signal(line_sem, inc=1, device_id=(section - 1, ctx), device_id_type=MESH)

    @pl.loop(2 * kv_heads - 2, 2 * kv_heads)
    def _(i):
        first_tick(i)

    @pl.loop(0, kv_heads)
    def _(i):
        h = visit(i)
        pair_copy(h).wait()
        own_top = parts[kv_heads + h, :, HD : HD + 1]
        own_totals = parts[kv_heads + h, :, 2 * HD - 1 :]
        pair_top = pair_arrived[h, :, HD : HD + 1]
        pair_totals = pair_arrived[h, :, 2 * HD - 1 :]
        top = jnp.maximum(own_top, pair_top)
        own_factor = jnp.exp2((own_top - top) * EXPONENT_SCALE)
        pair_factor = jnp.exp2((pair_top - top) * EXPONENT_SCALE)
        totals = own_factor * own_totals + pair_factor * pair_totals
        weighted = (
            own_factor * parts[kv_heads + h, :, :HD] + pair_factor * pair_arrived[h, :, :HD]
        )
        ship(0, h, top, totals, weighted)

    def cache_copies(h):
        from_slot, to_slot = 2 * kv_heads + h, 2 * h + core
        return (
            remote(
                keys.at[from_slot],
                keys.at[to_slot],
                cache_send_sem.at[h, 0],
                cache_recv_sem.at[h, 0],
                sibling,
            ),
            remote(
                values.at[from_slot, :, pl.ds(0, HD)],
                values.at[to_slot, :, pl.ds(0, HD)],
                cache_send_sem.at[h, 1],
                cache_recv_sem.at[h, 1],
                sibling,
            ),
        )

    def cache_arrivals(h):
        from_slot, to_slot = 2 * kv_heads + h, 2 * h + other
        return (
            remote(
                keys.at[from_slot],
                keys.at[to_slot],
                cache_send_sem.at[h, 0],
                cache_recv_sem.at[h, 0],
                sibling,
            ),
            remote(
                values.at[from_slot, :, pl.ds(0, HD)],
                values.at[to_slot, :, pl.ds(0, HD)],
                cache_send_sem.at[h, 1],
                cache_recv_sem.at[h, 1],
                sibling,
            ),
        )

    for h in range(kv_heads):
        for copy in cache_copies(h):
            copy.start()

    for copy in late:
        copy.wait()
    frames_copy.wait()
    column = jnp.where(not_first, held_frames(section - 1), entering_frames())
    for side in range(2):
        mask = shown(pl.ds(side * stride, own_keys), column)
        span = slice(side * own_keys, (side + 1) * own_keys)
        bias[0:tokens, span] = mask
        bias[tokens : 2 * tokens, span] = mask

    combine(0, act[:, columns(core * n_chips + chip, chunk_columns)].astype(jnp.float32))

    def hand_copy(j):
        return remote(
            combined.at[0],
            handed.at[:, columns(chip, chunk_columns)],
            hand_send_sem.at[j],
            hand_recv_sem.at[chip],
            (section + 1, j * 2 + core),
        )

    def hand_arrival(j):
        return remote(
            combined.at[0],
            handed.at[:, columns(j, chunk_columns)],
            hand_send_sem.at[j],
            hand_recv_sem.at[j],
            (section - 1, j * 2 + core),
        )

    @pl.when(not_last)
    def _():
        pl.semaphore_wait(line_sem, 1)

        @pl.loop(0, n_chips)
        def _(k):
            hand_copy(far_first(k)).start()

    def incoming(span):
        return jnp.where(
            not_first, handed[:, span].astype(jnp.float32), fresh[:, span].astype(jnp.float32)
        )

    for h in range(kv_heads):
        for copy in cache_arrivals(h):
            copy.wait()

    @pl.loop(0, kv_heads)
    def _(i):
        h = (chip // chunks_per_head + i) % kv_heads

        @pl.when(not_first)
        def _():
            for q in range(chunks_per_head):
                hand_arrival(h * chunks_per_head + q).wait_recv()

        span = columns(h, GROUP * HD)
        head_gain = gain[:, columns(core * kv_heads + h, GROUP * HD)]
        both = pl.ds(2 * h, 2)
        top, product = attend(
            queries_of(incoming(span), head_gain),
            keys[both].reshape(2 * own_keys, HD),
            values[both].reshape(2 * own_keys, 2 * HD),
            bias[...],
        )
        ship(1, h, top, product[:, HD:], product[:, :HD])

    combine(1, incoming(columns(chip, chunk_columns)))

    def result_columns(half, j):
        return columns(half * n_chips + j, chunk_columns)

    def out_copy(j):
        return remote(
            combined.at[1],
            out_ref.at[:, result_columns(core, chip)],
            out_send_sem.at[j],
            out_recv_sem.at[chip],
            in_line(j),
        )

    def out_arrival(j):
        return remote(
            combined.at[1],
            out_ref.at[:, result_columns(core, j)],
            out_send_sem.at[j],
            out_recv_sem.at[j],
            in_line(j),
        )

    def cross_copy(j, half):
        return remote(
            out_ref.at[:, result_columns(half, j)],
            out_ref.at[:, result_columns(half, j)],
            cross_send_sem.at[j],
            cross_recv_sem.at[j],
            sibling,
        )

    @pl.loop(0, n_chips - 1)
    def _(k):
        out_copy(far_first(k)).start()

    out_ref[:, result_columns(core, chip)] = combined[1]
    cross_copy(chip, core).start()

    @pl.loop(0, n_chips - 1)
    def _(k):
        j = far_first(n_chips - 2 - k)
        out_arrival(j).wait_recv()
        cross_copy(j, core).start()

    @pl.loop(0, n_chips)
    def _(j):
        @pl.when(not_last)
        def _():
            hand_copy(j).wait_send()

        @pl.when(j != chip)
        def _():
            out_copy(j).wait_send()

    @pl.loop(0, n_chips)
    def _(j):
        cross_copy(j, other).wait_recv()
        cross_copy(j, core).wait_send()


def attention(n_sections, n_chips, act, act_frames, fresh, fresh_frames, gain, keys, values, key_frames):
    tokens, width = act.shape
    own_keys = keys.shape[0]
    plane = width // 2
    kv_heads = plane // (GROUP * HD)
    chunk_columns = plane // n_chips
    packet_rows = chunk_columns // HD * tokens + STAT_ROWS
    dma = pltpu.SemaphoreType.DMA
    operands = [
        pltpu.with_memory_space_constraint(x, pltpu.HBM)
        for x in (act, act_frames, fresh, fresh_frames, gain, keys, values, key_frames)
    ]
    return pl.pallas_call(
        functools.partial(kernel, n_sections, n_chips),
        out_shape=jax.ShapeDtypeStruct((tokens, width), jnp.bfloat16),
        in_specs=[pl.BlockSpec(memory_space=pltpu.HBM)] * 8,
        out_specs=pl.BlockSpec(memory_space=pltpu.VMEM),
        scratch_shapes=[
            pltpu.VMEM((tokens, width), jnp.bfloat16),
            pltpu.VMEM((tokens, plane), jnp.bfloat16),
            pltpu.VMEM(act_frames.shape, jnp.int32),
            pltpu.VMEM(fresh_frames.shape, jnp.int32),
            pltpu.VMEM((1, width), jnp.float32),
            pltpu.VMEM((2 * frames_stride(own_keys),), jnp.int32),
            pltpu.VMEM((3 * kv_heads, own_keys, HD), jnp.bfloat16),
            pltpu.VMEM((3 * kv_heads, own_keys, 2 * HD), jnp.bfloat16),
            pltpu.VMEM((2 * tokens, 2 * own_keys), jnp.float32),
            pltpu.VMEM((2 * kv_heads, GROUP * tokens, 2 * HD), jnp.float32),
            pltpu.VMEM((kv_heads, GROUP * tokens, 2 * HD), jnp.float32),
            pltpu.VMEM((2, n_chips, packet_rows, HD), jnp.bfloat16),
            pltpu.VMEM((2, n_chips, packet_rows, HD), jnp.bfloat16),
            pltpu.VMEM((2, tokens, chunk_columns), jnp.bfloat16),
            pltpu.VMEM((tokens, plane), jnp.bfloat16),
            dma((6,)),
            dma((2 * kv_heads,)),
            dma((2 * kv_heads,)),
            dma((kv_heads,)),
            dma((kv_heads,)),
            dma((kv_heads, 2)),
            dma((kv_heads, 2)),
            dma,
            dma,
            dma((2, n_chips)),
            dma((2, n_chips)),
            dma((n_chips,)),
            dma((n_chips,)),
            dma((n_chips,)),
            dma((n_chips,)),
            dma((n_chips,)),
            dma((n_chips,)),
            pltpu.SemaphoreType.REGULAR,
        ],
        compiler_params=pltpu.CompilerParams(
            collective_id=0, has_side_effects=True, vmem_limit_bytes=48 * 2**20
        ),
        name="two_ticks",
    )(*operands)


def solution(mesh):
    n_sections, n_chips = mesh.shape["section"], mesh.shape["ctx"] // 2

    def body(act, act_frames, fresh, fresh_frames, gain, keys, values, key_frames):
        result = attention(
            n_sections,
            n_chips,
            act[0],
            act_frames.T,
            fresh,
            fresh_frames[None],
            gain,
            keys[0],
            values[0],
            key_frames,
        )
        return result[None]

    placed = (
        P("section", None, None),
        P(),
        P(),
        P(),
        P("section", None),
        P("section", "ctx", None),
        P("section", "ctx", None),
        P("ctx"),
    )
    return jax.shard_map(
        body, mesh=mesh, in_specs=placed, out_specs=P("section", None, None), check_vma=False
    )
```

```python
import functools
import math

import jax
import jax.numpy as jnp
from jax import lax
from jax.experimental import pallas as pl
from jax.experimental.pallas import tpu as pltpu
from jax.sharding import PartitionSpec as P

HD = 128
GROUP = 8
EPSILON = 1e-05
MASKED = -1e30
MESH = pl.DeviceIdType.MESH
EXPONENT_SCALE = HD**-0.5 * math.log2(math.e)
STAT_ROWS = 16
FARTHEST_FIRST = (2, 1, 3, 0)
NEAREST_FIRST = ((0, 3), (2, 1))


def frames_stride(count):
    return -(-count // 1024) * 1024


def remote(src, dst, send_sem, recv_sem, device):
    return pltpu.make_async_remote_copy(
        src_ref=src,
        dst_ref=dst,
        send_sem=send_sem,
        recv_sem=recv_sem,
        device_id=device,
        device_id_type=MESH,
    )


def kernel(
    n_sections,
    n_chips,
    act_hbm,
    act_frames_hbm,
    fresh_hbm,
    fresh_frames_hbm,
    gain_hbm,
    keys_hbm,
    values_hbm,
    key_frames_hbm,
    out_ref,
    act,
    fresh,
    act_frames,
    fresh_frames,
    gain,
    key_frames,
    keys,
    values,
    bias,
    parts,
    pair_arrived,
    sent,
    arrived,
    combined,
    handed,
    local_sem,
    keys_sem,
    values_sem,
    pair_send_sem,
    pair_recv_sem,
    cache_send_sem,
    cache_recv_sem,
    frames_send_sem,
    frames_recv_sem,
    part_send_sem,
    part_recv_sem,
    hand_send_sem,
    hand_recv_sem,
    out_send_sem,
    out_recv_sem,
    cross_send_sem,
    cross_recv_sem,
    line_sem,
):
    tokens = act.shape[0]
    own_keys = keys_hbm.shape[0]
    plane = fresh.shape[1]
    kv_heads = plane // (GROUP * HD)
    head_rows = GROUP * tokens
    chunk_columns = plane // n_chips
    heads_in_chunk = chunk_columns // HD
    chunk_rows = heads_in_chunk * tokens
    chunks_per_head = head_rows // chunk_rows

    section = lax.axis_index("section")
    ctx = lax.axis_index("ctx")
    chip, core = ctx // 2, ctx % 2
    other = 1 - core
    sibling = (section, chip * 2 + other)
    not_first = section != 0
    not_last = section != n_sections - 1

    def in_line(j):
        return (section, j * 2 + core)

    def columns(j, width):
        return pl.ds(pl.multiple_of(j * width, width), width)

    def far_first(k):
        half = n_chips // 2
        step = jnp.where(k % 2 == 1, half - (k + 1) // 2, half + k // 2)
        return (chip + step) % n_chips

    def slot_of(own, h):
        return 2 * h + core if own else 2 * kv_heads + h

    def head_at(step):
        return (chip // chunks_per_head + step) % kv_heads

    def loads(own, step):
        h = head_at(step)
        span = columns((core if own else other) * kv_heads + h, HD)
        slot, i = slot_of(own, h), own * kv_heads + step
        return (
            pltpu.make_async_copy(keys_hbm.at[:, span], keys.at[slot], keys_sem.at[i]),
            pltpu.make_async_copy(
                values_hbm.at[:, span], values.at[slot, :, pl.ds(0, HD)], values_sem.at[i]
            ),
        )

    stride = frames_stride(own_keys)
    own_frames = pl.ds(pl.multiple_of(core * stride, stride), own_keys)
    small = [
        pltpu.make_async_copy(act_hbm, act, local_sem.at[0]),
        pltpu.make_async_copy(act_frames_hbm, act_frames, local_sem.at[1]),
        pltpu.make_async_copy(gain_hbm, gain, local_sem.at[2]),
        pltpu.make_async_copy(key_frames_hbm, key_frames.at[own_frames], local_sem.at[3]),
    ]
    late = [
        pltpu.make_async_copy(fresh_hbm.at[:, columns(core, plane)], fresh, local_sem.at[4]),
        pltpu.make_async_copy(fresh_frames_hbm, fresh_frames, local_sem.at[5]),
    ]
    for copy in small:
        copy.start()

    barrier = pltpu.get_barrier_semaphore()
    pl.semaphore_signal(barrier, inc=1, device_id=sibling, device_id_type=MESH)

    @pl.loop(0, n_chips - 1)
    def _(k):
        pl.semaphore_signal(barrier, inc=1, device_id=in_line(far_first(k)), device_id_type=MESH)

    @pl.when(not_first)
    def _():
        pl.semaphore_signal(barrier, inc=1, device_id=(section - 1, ctx), device_id_type=MESH)

    @pl.when(not_last)
    def _():
        pl.semaphore_signal(barrier, inc=1, device_id=(section + 1, ctx), device_id_type=MESH)

    for own in (0, 1):
        for step in FARTHEST_FIRST:
            for copy in loads(own, step):
                copy.start()
    for copy in late:
        copy.start()
    for slot in range(values.shape[0]):
        values[slot, :, HD:] = jnp.ones((own_keys, HD), values.dtype)
    for copy in small:
        copy.wait()

    def held_frames(s):
        lanes = lax.broadcasted_iota(jnp.int32, act_frames.shape, 1)
        spread = act_frames[...].astype(jnp.float32)
        return jnp.sum(jnp.where(lanes == s, spread, 0.0), axis=1, keepdims=True)

    def entering_frames():
        rows = lax.broadcasted_iota(jnp.int32, (tokens, tokens), 0)
        lanes = lax.broadcasted_iota(jnp.int32, (tokens, tokens), 1)
        spread = jnp.broadcast_to(fresh_frames[...], (tokens, tokens)).astype(jnp.float32)
        return jnp.sum(jnp.where(rows == lanes, spread, 0.0), axis=1, keepdims=True)

    def shown(frames, column):
        row = key_frames[frames].astype(jnp.float32)[None]
        return jnp.where(row <= column, 0.0, MASKED)

    def queries_of(hidden, head_gain):
        rows = []
        for g in range(GROUP):
            span = slice(g * HD, (g + 1) * HD)
            x = hidden[:, span]
            mean = jnp.mean(x * x, axis=1, keepdims=True)
            rows.append(x * lax.rsqrt(mean + EPSILON) * head_gain[:, span])
        return jnp.concatenate(rows, axis=0).astype(jnp.bfloat16)

    def attend(queries, head_keys, head_values, mask):
        scores = lax.dot_general(
            queries, head_keys, (((1,), (1,)), ((), ())), preferred_element_type=jnp.float32
        )
        block = 2 * tokens
        maxima, probs = [], []
        for g in range(head_rows // block):
            part = scores[g * block : (g + 1) * block] + mask
            top = jnp.max(part, axis=1, keepdims=True)
            maxima.append(top)
            probs.append(jnp.exp2((part - top) * EXPONENT_SCALE).astype(jnp.bfloat16))
        product = lax.dot_general(
            jnp.concatenate(probs, axis=0),
            head_values,
            (((1,), (0,)), ((), ())),
            preferred_element_type=jnp.float32,
        )
        return jnp.concatenate(maxima, axis=0), product

    def part_copy(tick, j):
        return remote(
            sent.at[tick, j],
            arrived.at[tick, chip],
            part_send_sem.at[tick, j],
            part_recv_sem.at[tick, chip],
            in_line(j),
        )

    def part_arrival(tick, j):
        return remote(
            sent.at[tick, j],
            arrived.at[tick, j],
            part_send_sem.at[tick, j],
            part_recv_sem.at[tick, j],
            in_line(j),
        )

    def ship(tick, step, top, totals, weighted):
        h = head_at(step)
        lanes = lax.broadcasted_iota(jnp.int32, (chunk_rows, HD), 1)
        packets = []
        for q in range(chunks_per_head):
            span = slice(q * chunk_rows, (q + 1) * chunk_rows)
            stats = jnp.where(lanes % 2 == 0, top[span], totals[span])
            high = stats.astype(jnp.bfloat16).astype(jnp.float32)
            middle = (stats - high).astype(jnp.bfloat16).astype(jnp.float32)
            low = stats - high - middle
            terms = jnp.where(lanes < 2, high, jnp.where(lanes < 4, middle, low))
            terms = jnp.concatenate(
                [terms, jnp.ones((HD - chunk_rows, HD), jnp.float32)], axis=0
            ).T[:STAT_ROWS]
            packets.append(jnp.concatenate([weighted[span], terms], axis=0))
        if step:
            for q in range(chunks_per_head):
                j = h * chunks_per_head + q
                sent[tick, j] = packets[q].astype(jnp.bfloat16)
                part_copy(tick, j).start()
        else:
            even = chip % 2 == 0
            arrived[tick, chip] = jnp.where(even, packets[0], packets[1]).astype(jnp.bfloat16)
            j = chip + jnp.where(even, 1, -1)
            sent[tick, j] = jnp.where(even, packets[1], packets[0]).astype(jnp.bfloat16)
            part_copy(tick, j).start()

    def combine(tick, residual):
        @pl.loop(0, n_chips - 1)
        def _(k):
            part_arrival(tick, far_first(n_chips - 2 - k)).wait()

        stats = arrived[tick, :, chunk_rows:, :].astype(jnp.float32)
        tops = stats[:, 0] + stats[:, 2] + stats[:, 4]
        totals = stats[:, 1] + stats[:, 3] + stats[:, 5]
        overall = jnp.max(tops, axis=0, keepdims=True)
        factors = jnp.exp2((tops - overall) * EXPONENT_SCALE)
        factors = factors / jnp.sum(factors * totals, axis=0, keepdims=True)
        factors = jnp.concatenate(
            [factors, jnp.zeros((HD - n_chips, HD), jnp.float32)], axis=0
        ).T
        attended = jnp.zeros((chunk_rows, HD), jnp.float32)
        for j in range(n_chips):
            weighted = arrived[tick, j, :chunk_rows].astype(jnp.float32)
            attended += factors[:chunk_rows, j : j + 1] * weighted
        for g in range(heads_in_chunk):
            lanes = slice(g * HD, (g + 1) * HD)
            combined[tick, :, lanes] = (
                residual[:, lanes] + attended[g * tokens : (g + 1) * tokens]
            ).astype(jnp.bfloat16)

    mask = shown(own_frames, held_frames(section))
    bias[0:tokens, 0:own_keys] = mask
    bias[tokens : 2 * tokens, 0:own_keys] = mask
    pair_lanes = lax.broadcasted_iota(jnp.int32, (head_rows, HD), 1)

    def first_tick(own):
        for step in FARTHEST_FIRST:
            for copy in loads(own, step):
                copy.wait()
        for step in FARTHEST_FIRST:
            h = head_at(step)
            span = columns((core if own else other) * kv_heads + h, GROUP * HD)
            slot = slot_of(own, h)
            queries = queries_of(act[:, span].astype(jnp.float32), gain[:, span])
            top, product = attend(queries, keys[slot], values[slot], bias[:, 0:own_keys])
            place = own * kv_heads + h
            parts[place, :, :HD] = product[:, :HD]
            parts[place, :, HD:] = jnp.where(pair_lanes < HD // 2, top, product[:, HD:])

    first_tick(0)
    pl.semaphore_wait(barrier, n_chips + not_first.astype(jnp.int32) + not_last.astype(jnp.int32))

    def pair_copy(h):
        return remote(
            parts.at[h], pair_arrived.at[h], pair_send_sem.at[h], pair_recv_sem.at[h], sibling
        )

    for step in FARTHEST_FIRST:
        pair_copy(head_at(step)).start()

    frames_copy = remote(
        key_frames_hbm, key_frames.at[own_frames], frames_send_sem, frames_recv_sem, sibling
    )
    frames_copy.start()

    @pl.when(not_first)
    def _():
        pl.semaphore_signal(line_sem, inc=1, device_id=(section - 1, ctx), device_id_type=MESH)

    first_tick(1)

    for step in FARTHEST_FIRST:
        h = head_at(step)
        pair_copy(h).wait()
        own_top = parts[kv_heads + h, :, HD : HD + 1]
        own_totals = parts[kv_heads + h, :, 2 * HD - 1 :]
        pair_top = pair_arrived[h, :, HD : HD + 1]
        pair_totals = pair_arrived[h, :, 2 * HD - 1 :]
        top = jnp.maximum(own_top, pair_top)
        own_factor = jnp.exp2((own_top - top) * EXPONENT_SCALE)
        pair_factor = jnp.exp2((pair_top - top) * EXPONENT_SCALE)
        totals = own_factor * own_totals + pair_factor * pair_totals
        weighted = (
            own_factor * parts[kv_heads + h, :, :HD] + pair_factor * pair_arrived[h, :, :HD]
        )
        ship(0, step, top, totals, weighted)

    def cache_copies(h):
        from_slot, to_slot = 2 * kv_heads + h, 2 * h + core
        return (
            remote(
                keys.at[from_slot],
                keys.at[to_slot],
                cache_send_sem.at[h, 0],
                cache_recv_sem.at[h, 0],
                sibling,
            ),
            remote(
                values.at[from_slot, :, pl.ds(0, HD)],
                values.at[to_slot, :, pl.ds(0, HD)],
                cache_send_sem.at[h, 1],
                cache_recv_sem.at[h, 1],
                sibling,
            ),
        )

    def cache_arrivals(h):
        from_slot, to_slot = 2 * kv_heads + h, 2 * h + other
        return (
            remote(
                keys.at[from_slot],
                keys.at[to_slot],
                cache_send_sem.at[h, 0],
                cache_recv_sem.at[h, 0],
                sibling,
            ),
            remote(
                values.at[from_slot, :, pl.ds(0, HD)],
                values.at[to_slot, :, pl.ds(0, HD)],
                cache_send_sem.at[h, 1],
                cache_recv_sem.at[h, 1],
                sibling,
            ),
        )

    for h in range(kv_heads):
        for copy in cache_copies(h):
            copy.start()

    for copy in late:
        copy.wait()
    frames_copy.wait()
    column = jnp.where(not_first, held_frames(section - 1), entering_frames())
    for side in range(2):
        mask = shown(pl.ds(side * stride, own_keys), column)
        span = slice(side * own_keys, (side + 1) * own_keys)
        bias[0:tokens, span] = mask
        bias[tokens : 2 * tokens, span] = mask

    combine(0, act[:, columns(core * n_chips + chip, chunk_columns)].astype(jnp.float32))

    def hand_copy(j):
        return remote(
            combined.at[0],
            handed.at[:, columns(chip, chunk_columns)],
            hand_send_sem.at[j],
            hand_recv_sem.at[chip],
            (section + 1, j * 2 + core),
        )

    def hand_arrival(j):
        return remote(
            combined.at[0],
            handed.at[:, columns(j, chunk_columns)],
            hand_send_sem.at[j],
            hand_recv_sem.at[j],
            (section - 1, j * 2 + core),
        )

    @pl.when(not_last)
    def _():
        pl.semaphore_wait(line_sem, 1)

        @pl.loop(0, n_chips)
        def _(k):
            hand_copy(far_first(k)).start()

    def incoming(span):
        return jnp.where(
            not_first, handed[:, span].astype(jnp.float32), fresh[:, span].astype(jnp.float32)
        )

    for h in range(kv_heads):
        for copy in cache_arrivals(h):
            copy.wait()

    for steps in NEAREST_FIRST:

        @pl.when(not_first)
        def _(steps=steps):
            for step in steps:
                for q in range(chunks_per_head):
                    hand_arrival(head_at(step) * chunks_per_head + q).wait_recv()

        results = []
        for step in steps:
            h = head_at(step)
            head_gain = gain[:, columns(core * kv_heads + h, GROUP * HD)]
            both = pl.ds(2 * h, 2)
            results.append(
                attend(
                    queries_of(incoming(columns(h, GROUP * HD)), head_gain),
                    keys[both].reshape(2 * own_keys, HD),
                    values[both].reshape(2 * own_keys, 2 * HD),
                    bias[...],
                )
            )
        for step, (top, product) in zip(steps, results):
            ship(1, step, top, product[:, HD:], product[:, :HD])

    combine(1, incoming(columns(chip, chunk_columns)))

    def result_columns(half, j):
        return columns(half * n_chips + j, chunk_columns)

    def out_copy(j):
        return remote(
            combined.at[1],
            out_ref.at[:, result_columns(core, chip)],
            out_send_sem.at[j],
            out_recv_sem.at[chip],
            in_line(j),
        )

    def out_arrival(j):
        return remote(
            combined.at[1],
            out_ref.at[:, result_columns(core, j)],
            out_send_sem.at[j],
            out_recv_sem.at[j],
            in_line(j),
        )

    def cross_copy(j, half):
        return remote(
            out_ref.at[:, result_columns(half, j)],
            out_ref.at[:, result_columns(half, j)],
            cross_send_sem.at[j],
            cross_recv_sem.at[j],
            sibling,
        )

    @pl.loop(0, n_chips - 1)
    def _(k):
        out_copy(far_first(k)).start()

    out_ref[:, result_columns(core, chip)] = combined[1]
    cross_copy(chip, core).start()

    @pl.loop(0, n_chips - 1)
    def _(k):
        j = far_first(n_chips - 2 - k)
        out_arrival(j).wait_recv()
        cross_copy(j, core).start()

    @pl.loop(0, n_chips)
    def _(j):
        @pl.when(not_last)
        def _():
            hand_copy(j).wait_send()

        @pl.when(j != chip)
        def _():
            out_copy(j).wait_send()

    @pl.loop(0, n_chips)
    def _(j):
        cross_copy(j, other).wait_recv()
        cross_copy(j, core).wait_send()


def attention(n_sections, n_chips, act, act_frames, fresh, fresh_frames, gain, keys, values, key_frames):
    tokens, width = act.shape
    own_keys = keys.shape[0]
    plane = width // 2
    kv_heads = plane // (GROUP * HD)
    chunk_columns = plane // n_chips
    packet_rows = chunk_columns // HD * tokens + STAT_ROWS
    dma = pltpu.SemaphoreType.DMA
    operands = [
        pltpu.with_memory_space_constraint(x, pltpu.HBM)
        for x in (act, act_frames, fresh, fresh_frames, gain, keys, values, key_frames)
    ]
    return pl.pallas_call(
        functools.partial(kernel, n_sections, n_chips),
        out_shape=jax.ShapeDtypeStruct((tokens, width), jnp.bfloat16),
        in_specs=[pl.BlockSpec(memory_space=pltpu.HBM)] * 8,
        out_specs=pl.BlockSpec(memory_space=pltpu.VMEM),
        scratch_shapes=[
            pltpu.VMEM((tokens, width), jnp.bfloat16),
            pltpu.VMEM((tokens, plane), jnp.bfloat16),
            pltpu.VMEM(act_frames.shape, jnp.int32),
            pltpu.VMEM(fresh_frames.shape, jnp.int32),
            pltpu.VMEM((1, width), jnp.float32),
            pltpu.VMEM((2 * frames_stride(own_keys),), jnp.int32),
            pltpu.VMEM((3 * kv_heads, own_keys, HD), jnp.bfloat16),
            pltpu.VMEM((3 * kv_heads, own_keys, 2 * HD), jnp.bfloat16),
            pltpu.VMEM((2 * tokens, 2 * own_keys), jnp.float32),
            pltpu.VMEM((2 * kv_heads, GROUP * tokens, 2 * HD), jnp.float32),
            pltpu.VMEM((kv_heads, GROUP * tokens, 2 * HD), jnp.float32),
            pltpu.VMEM((2, n_chips, packet_rows, HD), jnp.bfloat16),
            pltpu.VMEM((2, n_chips, packet_rows, HD), jnp.bfloat16),
            pltpu.VMEM((2, tokens, chunk_columns), jnp.bfloat16),
            pltpu.VMEM((tokens, plane), jnp.bfloat16),
            dma((6,)),
            dma((2 * kv_heads,)),
            dma((2 * kv_heads,)),
            dma((kv_heads,)),
            dma((kv_heads,)),
            dma((kv_heads, 2)),
            dma((kv_heads, 2)),
            dma,
            dma,
            dma((2, n_chips)),
            dma((2, n_chips)),
            dma((n_chips,)),
            dma((n_chips,)),
            dma((n_chips,)),
            dma((n_chips,)),
            dma((n_chips,)),
            dma((n_chips,)),
            pltpu.SemaphoreType.REGULAR,
        ],
        compiler_params=pltpu.CompilerParams(
            collective_id=0, has_side_effects=True, vmem_limit_bytes=48 * 2**20
        ),
        name="two_ticks",
    )(*operands)


def solution(mesh):
    n_sections, n_chips = mesh.shape["section"], mesh.shape["ctx"] // 2

    def body(act, act_frames, fresh, fresh_frames, gain, keys, values, key_frames):
        result = attention(
            n_sections,
            n_chips,
            act[0],
            act_frames.T,
            fresh,
            fresh_frames[None],
            gain,
            keys[0],
            values[0],
            key_frames,
        )
        return result[None]

    placed = (
        P("section", None, None),
        P(),
        P(),
        P(),
        P("section", None),
        P("section", "ctx", None),
        P("section", "ctx", None),
        P("ctx"),
    )
    return jax.shard_map(
        body, mesh=mesh, in_specs=placed, out_specs=P("section", None, None), check_vma=False
    )
```

```python
import functools
import math

import jax
import jax.numpy as jnp
from jax import lax
from jax.experimental import pallas as pl
from jax.experimental.pallas import tpu as pltpu
from jax.sharding import PartitionSpec as P

HD = 128
GROUP = 8
EPSILON = 1e-05
MASKED = -1e30
MESH = pl.DeviceIdType.MESH
EXPONENT_SCALE = HD**-0.5 * math.log2(math.e)
STAT_ROWS = 16
FARTHEST_FIRST = (2, 1, 3, 0)
SECOND_TICK_STEPS = ((2, 1), (3, 0))


def frames_stride(count):
    return -(-count // 1024) * 1024


def remote(src, dst, send_sem, recv_sem, device):
    return pltpu.make_async_remote_copy(
        src_ref=src,
        dst_ref=dst,
        send_sem=send_sem,
        recv_sem=recv_sem,
        device_id=device,
        device_id_type=MESH,
    )


def kernel(
    n_sections,
    n_chips,
    act_hbm,
    act_frames_hbm,
    fresh_hbm,
    fresh_frames_hbm,
    gain_hbm,
    keys_hbm,
    values_hbm,
    key_frames_hbm,
    out_ref,
    act,
    fresh,
    act_frames,
    fresh_frames,
    gain,
    key_frames,
    keys,
    values,
    bias,
    parts,
    pair_arrived,
    sent,
    arrived,
    combined,
    handed,
    local_sem,
    keys_sem,
    values_sem,
    pair_send_sem,
    pair_recv_sem,
    cache_send_sem,
    cache_recv_sem,
    frames_send_sem,
    frames_recv_sem,
    part_send_sem,
    part_recv_sem,
    hand_send_sem,
    hand_recv_sem,
    out_send_sem,
    out_recv_sem,
    cross_send_sem,
    cross_recv_sem,
    line_sem,
):
    tokens = act.shape[0]
    own_keys = keys_hbm.shape[0]
    plane = fresh.shape[1]
    kv_heads = plane // (GROUP * HD)
    head_rows = GROUP * tokens
    chunk_columns = plane // n_chips
    heads_in_chunk = chunk_columns // HD
    chunk_rows = heads_in_chunk * tokens
    chunks_per_head = head_rows // chunk_rows

    section = lax.axis_index("section")
    ctx = lax.axis_index("ctx")
    chip, core = ctx // 2, ctx % 2
    other = 1 - core
    sibling = (section, chip * 2 + other)
    not_first = section != 0
    not_last = section != n_sections - 1

    def in_line(j):
        return (section, j * 2 + core)

    def columns(j, width):
        return pl.ds(pl.multiple_of(j * width, width), width)

    def far_first(k):
        half = n_chips // 2
        step = jnp.where(k % 2 == 1, half - (k + 1) // 2, half + k // 2)
        return (chip + step) % n_chips

    def slot_of(own, h):
        return 2 * h + core if own else 2 * kv_heads + h

    def head_at(step):
        return (chip // chunks_per_head + step) % kv_heads

    def loads(own, step):
        h = head_at(step)
        span = columns((core if own else other) * kv_heads + h, HD)
        slot, i = slot_of(own, h), own * kv_heads + step
        return (
            pltpu.make_async_copy(keys_hbm.at[:, span], keys.at[slot], keys_sem.at[i]),
            pltpu.make_async_copy(
                values_hbm.at[:, span], values.at[slot, :, pl.ds(0, HD)], values_sem.at[i]
            ),
        )

    stride = frames_stride(own_keys)
    own_frames = pl.ds(pl.multiple_of(core * stride, stride), own_keys)
    small = [
        pltpu.make_async_copy(act_hbm, act, local_sem.at[0]),
        pltpu.make_async_copy(act_frames_hbm, act_frames, local_sem.at[1]),
        pltpu.make_async_copy(gain_hbm, gain, local_sem.at[2]),
        pltpu.make_async_copy(key_frames_hbm, key_frames.at[own_frames], local_sem.at[3]),
    ]
    late = [
        pltpu.make_async_copy(fresh_hbm.at[:, columns(core, plane)], fresh, local_sem.at[4]),
        pltpu.make_async_copy(fresh_frames_hbm, fresh_frames, local_sem.at[5]),
    ]
    for copy in small:
        copy.start()

    barrier = pltpu.get_barrier_semaphore()
    pl.semaphore_signal(barrier, inc=1, device_id=sibling, device_id_type=MESH)

    @pl.loop(0, n_chips - 1)
    def _(k):
        pl.semaphore_signal(barrier, inc=1, device_id=in_line(far_first(k)), device_id_type=MESH)

    @pl.when(not_first)
    def _():
        pl.semaphore_signal(barrier, inc=1, device_id=(section - 1, ctx), device_id_type=MESH)

    @pl.when(not_last)
    def _():
        pl.semaphore_signal(barrier, inc=1, device_id=(section + 1, ctx), device_id_type=MESH)

    for own in (0, 1):
        for step in FARTHEST_FIRST:
            for copy in loads(own, step):
                copy.start()
    for copy in late:
        copy.start()
    for slot in range(values.shape[0]):
        values[slot, :, HD:] = jnp.ones((own_keys, HD), values.dtype)
    for copy in small:
        copy.wait()

    def held_frames(s):
        lanes = lax.broadcasted_iota(jnp.int32, act_frames.shape, 1)
        spread = act_frames[...].astype(jnp.float32)
        return jnp.sum(jnp.where(lanes == s, spread, 0.0), axis=1, keepdims=True)

    def entering_frames():
        rows = lax.broadcasted_iota(jnp.int32, (tokens, tokens), 0)
        lanes = lax.broadcasted_iota(jnp.int32, (tokens, tokens), 1)
        spread = jnp.broadcast_to(fresh_frames[...], (tokens, tokens)).astype(jnp.float32)
        return jnp.sum(jnp.where(rows == lanes, spread, 0.0), axis=1, keepdims=True)

    def shown(frames, column):
        row = key_frames[frames].astype(jnp.float32)[None]
        return jnp.where(row <= column, 0.0, MASKED)

    def queries_of(hidden, head_gain):
        rows = []
        for g in range(GROUP):
            span = slice(g * HD, (g + 1) * HD)
            x = hidden[:, span]
            mean = jnp.mean(x * x, axis=1, keepdims=True)
            rows.append(x * lax.rsqrt(mean + EPSILON) * head_gain[:, span])
        return jnp.concatenate(rows, axis=0).astype(jnp.bfloat16)

    def attend(queries, head_keys, head_values, mask):
        scores = lax.dot_general(
            queries, head_keys, (((1,), (1,)), ((), ())), preferred_element_type=jnp.float32
        )
        block = 2 * tokens
        maxima, probs = [], []
        for g in range(head_rows // block):
            part = scores[g * block : (g + 1) * block] + mask
            top = jnp.max(part, axis=1, keepdims=True)
            maxima.append(top)
            probs.append(jnp.exp2((part - top) * EXPONENT_SCALE).astype(jnp.bfloat16))
        product = lax.dot_general(
            jnp.concatenate(probs, axis=0),
            head_values,
            (((1,), (0,)), ((), ())),
            preferred_element_type=jnp.float32,
        )
        return jnp.concatenate(maxima, axis=0), product

    def part_copy(tick, j):
        return remote(
            sent.at[tick, j],
            arrived.at[tick, chip],
            part_send_sem.at[tick, j],
            part_recv_sem.at[tick, chip],
            in_line(j),
        )

    def part_arrival(tick, j):
        return remote(
            sent.at[tick, j],
            arrived.at[tick, j],
            part_send_sem.at[tick, j],
            part_recv_sem.at[tick, j],
            in_line(j),
        )

    def ship(tick, step, top, totals, weighted):
        h = head_at(step)
        lanes = lax.broadcasted_iota(jnp.int32, (chunk_rows, HD), 1)
        packets = []
        for q in range(chunks_per_head):
            span = slice(q * chunk_rows, (q + 1) * chunk_rows)
            stats = jnp.where(lanes % 2 == 0, top[span], totals[span])
            high = stats.astype(jnp.bfloat16).astype(jnp.float32)
            middle = (stats - high).astype(jnp.bfloat16).astype(jnp.float32)
            low = stats - high - middle
            terms = jnp.where(lanes < 2, high, jnp.where(lanes < 4, middle, low))
            terms = jnp.concatenate(
                [terms, jnp.ones((HD - chunk_rows, HD), jnp.float32)], axis=0
            ).T[:STAT_ROWS]
            packets.append(jnp.concatenate([weighted[span], terms], axis=0))
        if step:
            for q in range(chunks_per_head):
                j = h * chunks_per_head + q
                sent[tick, j] = packets[q].astype(jnp.bfloat16)
                part_copy(tick, j).start()
        else:
            even = chip % 2 == 0
            arrived[tick, chip] = jnp.where(even, packets[0], packets[1]).astype(jnp.bfloat16)
            j = chip + jnp.where(even, 1, -1)
            sent[tick, j] = jnp.where(even, packets[1], packets[0]).astype(jnp.bfloat16)
            part_copy(tick, j).start()

    def combine(tick, residual):
        @pl.loop(0, n_chips - 1)
        def _(k):
            part_arrival(tick, far_first(n_chips - 2 - k)).wait()

        stats = arrived[tick, :, chunk_rows:, :].astype(jnp.float32)
        tops = stats[:, 0] + stats[:, 2] + stats[:, 4]
        totals = stats[:, 1] + stats[:, 3] + stats[:, 5]
        overall = jnp.max(tops, axis=0, keepdims=True)
        factors = jnp.exp2((tops - overall) * EXPONENT_SCALE)
        factors = factors / jnp.sum(factors * totals, axis=0, keepdims=True)
        factors = jnp.concatenate(
            [factors, jnp.zeros((HD - n_chips, HD), jnp.float32)], axis=0
        ).T
        attended = jnp.zeros((chunk_rows, HD), jnp.float32)
        for j in range(n_chips):
            weighted = arrived[tick, j, :chunk_rows].astype(jnp.float32)
            attended += factors[:chunk_rows, j : j + 1] * weighted
        for g in range(heads_in_chunk):
            lanes = slice(g * HD, (g + 1) * HD)
            combined[tick, :, lanes] = (
                residual[:, lanes] + attended[g * tokens : (g + 1) * tokens]
            ).astype(jnp.bfloat16)

    mask = shown(own_frames, held_frames(section))
    bias[0:tokens, 0:own_keys] = mask
    bias[tokens : 2 * tokens, 0:own_keys] = mask
    pair_lanes = lax.broadcasted_iota(jnp.int32, (head_rows, HD), 1)

    def first_tick(own):
        for step in FARTHEST_FIRST:
            for copy in loads(own, step):
                copy.wait()
        for step in FARTHEST_FIRST:
            h = head_at(step)
            span = columns((core if own else other) * kv_heads + h, GROUP * HD)
            slot = slot_of(own, h)
            queries = queries_of(act[:, span].astype(jnp.float32), gain[:, span])
            top, product = attend(queries, keys[slot], values[slot], bias[:, 0:own_keys])
            place = own * kv_heads + h
            parts[place, :, :HD] = product[:, :HD]
            parts[place, :, HD:] = jnp.where(pair_lanes < HD // 2, top, product[:, HD:])

    first_tick(0)
    pl.semaphore_wait(barrier, n_chips + not_first.astype(jnp.int32) + not_last.astype(jnp.int32))

    def pair_copy(h):
        return remote(
            parts.at[h], pair_arrived.at[h], pair_send_sem.at[h], pair_recv_sem.at[h], sibling
        )

    for step in FARTHEST_FIRST:
        pair_copy(head_at(step)).start()

    frames_copy = remote(
        key_frames_hbm, key_frames.at[own_frames], frames_send_sem, frames_recv_sem, sibling
    )
    frames_copy.start()

    @pl.when(not_first)
    def _():
        pl.semaphore_signal(line_sem, inc=1, device_id=(section - 1, ctx), device_id_type=MESH)

    first_tick(1)

    for step in FARTHEST_FIRST:
        h = head_at(step)
        pair_copy(h).wait()
        own_top = parts[kv_heads + h, :, HD : HD + 1]
        own_totals = parts[kv_heads + h, :, 2 * HD - 1 :]
        pair_top = pair_arrived[h, :, HD : HD + 1]
        pair_totals = pair_arrived[h, :, 2 * HD - 1 :]
        top = jnp.maximum(own_top, pair_top)
        own_factor = jnp.exp2((own_top - top) * EXPONENT_SCALE)
        pair_factor = jnp.exp2((pair_top - top) * EXPONENT_SCALE)
        totals = own_factor * own_totals + pair_factor * pair_totals
        weighted = (
            own_factor * parts[kv_heads + h, :, :HD] + pair_factor * pair_arrived[h, :, :HD]
        )
        ship(0, step, top, totals, weighted)

    def cache_copies(h):
        from_slot, to_slot = 2 * kv_heads + h, 2 * h + core
        return (
            remote(
                keys.at[from_slot],
                keys.at[to_slot],
                cache_send_sem.at[h, 0],
                cache_recv_sem.at[h, 0],
                sibling,
            ),
            remote(
                values.at[from_slot, :, pl.ds(0, HD)],
                values.at[to_slot, :, pl.ds(0, HD)],
                cache_send_sem.at[h, 1],
                cache_recv_sem.at[h, 1],
                sibling,
            ),
        )

    def cache_arrivals(h):
        from_slot, to_slot = 2 * kv_heads + h, 2 * h + other
        return (
            remote(
                keys.at[from_slot],
                keys.at[to_slot],
                cache_send_sem.at[h, 0],
                cache_recv_sem.at[h, 0],
                sibling,
            ),
            remote(
                values.at[from_slot, :, pl.ds(0, HD)],
                values.at[to_slot, :, pl.ds(0, HD)],
                cache_send_sem.at[h, 1],
                cache_recv_sem.at[h, 1],
                sibling,
            ),
        )

    for copy in late:
        copy.wait()
    frames_copy.wait()
    column = jnp.where(not_first, held_frames(section - 1), entering_frames())
    for side in range(2):
        mask = shown(pl.ds(side * stride, own_keys), column)
        span = slice(side * own_keys, (side + 1) * own_keys)
        bias[0:tokens, span] = mask
        bias[tokens : 2 * tokens, span] = mask

    combine(0, act[:, columns(core * n_chips + chip, chunk_columns)].astype(jnp.float32))

    def hand_copy(j):
        return remote(
            combined.at[0],
            handed.at[:, columns(chip, chunk_columns)],
            hand_send_sem.at[j],
            hand_recv_sem.at[chip],
            (section + 1, j * 2 + core),
        )

    def hand_arrival(j):
        return remote(
            combined.at[0],
            handed.at[:, columns(j, chunk_columns)],
            hand_send_sem.at[j],
            hand_recv_sem.at[j],
            (section - 1, j * 2 + core),
        )

    @pl.when(not_last)
    def _():
        pl.semaphore_wait(line_sem, 1)

        @pl.loop(0, n_chips)
        def _(k):
            hand_copy(far_first(k)).start()

    for h in range(kv_heads):
        for copy in cache_copies(h):
            copy.start()

    def incoming(span):
        return jnp.where(
            not_first, handed[:, span].astype(jnp.float32), fresh[:, span].astype(jnp.float32)
        )

    for h in range(kv_heads):
        for copy in cache_arrivals(h):
            copy.wait()

    for steps in SECOND_TICK_STEPS:

        @pl.when(not_first)
        def _(steps=steps):
            for step in steps:
                for q in range(chunks_per_head):
                    hand_arrival(head_at(step) * chunks_per_head + q).wait_recv()

        results = []
        for step in steps:
            h = head_at(step)
            head_gain = gain[:, columns(core * kv_heads + h, GROUP * HD)]
            both = pl.ds(2 * h, 2)
            results.append(
                attend(
                    queries_of(incoming(columns(h, GROUP * HD)), head_gain),
                    keys[both].reshape(2 * own_keys, HD),
                    values[both].reshape(2 * own_keys, 2 * HD),
                    bias[...],
                )
            )
        for step, (top, product) in zip(steps, results):
            ship(1, step, top, product[:, HD:], product[:, :HD])

    combine(1, incoming(columns(chip, chunk_columns)))

    def result_columns(half, j):
        return columns(half * n_chips + j, chunk_columns)

    def out_copy(j):
        return remote(
            combined.at[1],
            out_ref.at[:, result_columns(core, chip)],
            out_send_sem.at[j],
            out_recv_sem.at[chip],
            in_line(j),
        )

    def out_arrival(j):
        return remote(
            combined.at[1],
            out_ref.at[:, result_columns(core, j)],
            out_send_sem.at[j],
            out_recv_sem.at[j],
            in_line(j),
        )

    def cross_copy(j, half):
        return remote(
            out_ref.at[:, result_columns(half, j)],
            out_ref.at[:, result_columns(half, j)],
            cross_send_sem.at[j],
            cross_recv_sem.at[j],
            sibling,
        )

    @pl.loop(0, n_chips - 1)
    def _(k):
        out_copy(far_first(k)).start()

    out_ref[:, result_columns(core, chip)] = combined[1]
    cross_copy(chip, core).start()

    @pl.loop(0, n_chips - 1)
    def _(k):
        j = far_first(n_chips - 2 - k)
        out_arrival(j).wait_recv()
        cross_copy(j, core).start()

    @pl.loop(0, n_chips)
    def _(j):
        @pl.when(not_last)
        def _():
            hand_copy(j).wait_send()

        @pl.when(j != chip)
        def _():
            out_copy(j).wait_send()

    @pl.loop(0, n_chips)
    def _(j):
        cross_copy(j, other).wait_recv()
        cross_copy(j, core).wait_send()


def attention(n_sections, n_chips, act, act_frames, fresh, fresh_frames, gain, keys, values, key_frames):
    tokens, width = act.shape
    own_keys = keys.shape[0]
    plane = width // 2
    kv_heads = plane // (GROUP * HD)
    chunk_columns = plane // n_chips
    packet_rows = chunk_columns // HD * tokens + STAT_ROWS
    dma = pltpu.SemaphoreType.DMA
    operands = [
        pltpu.with_memory_space_constraint(x, pltpu.HBM)
        for x in (act, act_frames, fresh, fresh_frames, gain, keys, values, key_frames)
    ]
    return pl.pallas_call(
        functools.partial(kernel, n_sections, n_chips),
        out_shape=jax.ShapeDtypeStruct((tokens, width), jnp.bfloat16),
        in_specs=[pl.BlockSpec(memory_space=pltpu.HBM)] * 8,
        out_specs=pl.BlockSpec(memory_space=pltpu.VMEM),
        scratch_shapes=[
            pltpu.VMEM((tokens, width), jnp.bfloat16),
            pltpu.VMEM((tokens, plane), jnp.bfloat16),
            pltpu.VMEM(act_frames.shape, jnp.int32),
            pltpu.VMEM(fresh_frames.shape, jnp.int32),
            pltpu.VMEM((1, width), jnp.float32),
            pltpu.VMEM((2 * frames_stride(own_keys),), jnp.int32),
            pltpu.VMEM((3 * kv_heads, own_keys, HD), jnp.bfloat16),
            pltpu.VMEM((3 * kv_heads, own_keys, 2 * HD), jnp.bfloat16),
            pltpu.VMEM((2 * tokens, 2 * own_keys), jnp.float32),
            pltpu.VMEM((2 * kv_heads, GROUP * tokens, 2 * HD), jnp.float32),
            pltpu.VMEM((kv_heads, GROUP * tokens, 2 * HD), jnp.float32),
            pltpu.VMEM((2, n_chips, packet_rows, HD), jnp.bfloat16),
            pltpu.VMEM((2, n_chips, packet_rows, HD), jnp.bfloat16),
            pltpu.VMEM((2, tokens, chunk_columns), jnp.bfloat16),
            pltpu.VMEM((tokens, plane), jnp.bfloat16),
            dma((6,)),
            dma((2 * kv_heads,)),
            dma((2 * kv_heads,)),
            dma((kv_heads,)),
            dma((kv_heads,)),
            dma((kv_heads, 2)),
            dma((kv_heads, 2)),
            dma,
            dma,
            dma((2, n_chips)),
            dma((2, n_chips)),
            dma((n_chips,)),
            dma((n_chips,)),
            dma((n_chips,)),
            dma((n_chips,)),
            dma((n_chips,)),
            dma((n_chips,)),
            pltpu.SemaphoreType.REGULAR,
        ],
        compiler_params=pltpu.CompilerParams(
            collective_id=0, has_side_effects=True, vmem_limit_bytes=48 * 2**20
        ),
        name="two_ticks",
    )(*operands)


def solution(mesh):
    n_sections, n_chips = mesh.shape["section"], mesh.shape["ctx"] // 2

    def body(act, act_frames, fresh, fresh_frames, gain, keys, values, key_frames):
        result = attention(
            n_sections,
            n_chips,
            act[0],
            act_frames.T,
            fresh,
            fresh_frames[None],
            gain,
            keys[0],
            values[0],
            key_frames,
        )
        return result[None]

    placed = (
        P("section", None, None),
        P(),
        P(),
        P(),
        P("section", None),
        P("section", "ctx", None),
        P("section", "ctx", None),
        P("ctx"),
    )
    return jax.shard_map(
        body, mesh=mesh, in_specs=placed, out_specs=P("section", None, None), check_vma=False
    )
```

```python
import functools
import math

import jax
import jax.numpy as jnp
from jax import lax
from jax.experimental import pallas as pl
from jax.experimental.pallas import tpu as pltpu
from jax.sharding import PartitionSpec as P

HD = 128
GROUP = 8
EPSILON = 1e-05
MASKED = -1e30
MESH = pl.DeviceIdType.MESH
EXPONENT_SCALE = HD**-0.5 * math.log2(math.e)
STAT_ROWS = 16
FARTHEST_FIRST = (2, 1, 3, 0)
SECOND_TICK_STEPS = ((2, 1), (3, 0))


def frames_stride(count):
    return -(-count // 1024) * 1024


def remote(src, dst, send_sem, recv_sem, device):
    return pltpu.make_async_remote_copy(
        src_ref=src,
        dst_ref=dst,
        send_sem=send_sem,
        recv_sem=recv_sem,
        device_id=device,
        device_id_type=MESH,
    )


def kernel(
    n_sections,
    n_chips,
    act_hbm,
    act_frames_hbm,
    fresh_hbm,
    fresh_frames_hbm,
    gain_hbm,
    keys_hbm,
    values_hbm,
    key_frames_hbm,
    out_ref,
    act,
    fresh,
    act_frames,
    fresh_frames,
    gain,
    key_frames,
    keys,
    values,
    bias,
    parts,
    pair_arrived,
    sent,
    arrived,
    combined,
    handed,
    local_sem,
    keys_sem,
    values_sem,
    pair_send_sem,
    pair_recv_sem,
    cache_send_sem,
    cache_recv_sem,
    frames_send_sem,
    frames_recv_sem,
    part_send_sem,
    part_recv_sem,
    hand_send_sem,
    hand_recv_sem,
    out_send_sem,
    out_recv_sem,
    cross_send_sem,
    cross_recv_sem,
    line_sem,
):
    tokens = act.shape[0]
    own_keys = keys_hbm.shape[0]
    plane = fresh.shape[1]
    kv_heads = plane // (GROUP * HD)
    head_rows = GROUP * tokens
    chunk_columns = plane // n_chips
    heads_in_chunk = chunk_columns // HD
    chunk_rows = heads_in_chunk * tokens
    chunks_per_head = head_rows // chunk_rows

    section = lax.axis_index("section")
    ctx = lax.axis_index("ctx")
    chip, core = ctx // 2, ctx % 2
    other = 1 - core
    sibling = (section, chip * 2 + other)
    not_first = section != 0
    not_last = section != n_sections - 1

    def in_line(j):
        return (section, j * 2 + core)

    def columns(j, width):
        return pl.ds(pl.multiple_of(j * width, width), width)

    def far_first(k):
        half = n_chips // 2
        step = jnp.where(k % 2 == 1, half - (k + 1) // 2, half + k // 2)
        return (chip + step) % n_chips

    barrier = pltpu.get_barrier_semaphore()
    for k in range(n_chips - 1):
        pl.semaphore_signal(barrier, inc=1, device_id=in_line(far_first(k)), device_id_type=MESH)

    @pl.when(not_first)
    def _():
        pl.semaphore_signal(barrier, inc=1, device_id=(section - 1, ctx), device_id_type=MESH)

    @pl.when(not_last)
    def _():
        pl.semaphore_signal(barrier, inc=1, device_id=(section + 1, ctx), device_id_type=MESH)

    pl.semaphore_signal(barrier, inc=1, device_id=sibling, device_id_type=MESH)

    def slot_of(own, h):
        return 2 * h + core if own else 2 * kv_heads + h

    def head_at(step):
        return (chip // chunks_per_head + step) % kv_heads

    def loads(own, step):
        h = head_at(step)
        span = columns((core if own else other) * kv_heads + h, HD)
        slot, i = slot_of(own, h), own * kv_heads + step
        return (
            pltpu.make_async_copy(keys_hbm.at[:, span], keys.at[slot], keys_sem.at[i]),
            pltpu.make_async_copy(
                values_hbm.at[:, span], values.at[slot, :, pl.ds(0, HD)], values_sem.at[i]
            ),
        )

    stride = frames_stride(own_keys)
    own_frames = pl.ds(pl.multiple_of(core * stride, stride), own_keys)
    small = [
        pltpu.make_async_copy(act_hbm, act, local_sem.at[0]),
        pltpu.make_async_copy(act_frames_hbm, act_frames, local_sem.at[1]),
        pltpu.make_async_copy(gain_hbm, gain, local_sem.at[2]),
        pltpu.make_async_copy(key_frames_hbm, key_frames.at[own_frames], local_sem.at[3]),
    ]
    late = [
        pltpu.make_async_copy(fresh_hbm.at[:, columns(core, plane)], fresh, local_sem.at[4]),
        pltpu.make_async_copy(fresh_frames_hbm, fresh_frames, local_sem.at[5]),
    ]
    for copy in small:
        copy.start()

    for own in (0, 1):
        for step in FARTHEST_FIRST:
            for copy in loads(own, step):
                copy.start()
    for copy in late:
        copy.start()
    for slot in range(values.shape[0]):
        values[slot, :, HD:] = jnp.ones((own_keys, HD), values.dtype)
    for copy in small:
        copy.wait()

    def held_frames(s):
        lanes = lax.broadcasted_iota(jnp.int32, act_frames.shape, 1)
        spread = act_frames[...].astype(jnp.float32)
        return jnp.sum(jnp.where(lanes == s, spread, 0.0), axis=1, keepdims=True)

    def entering_frames():
        rows = lax.broadcasted_iota(jnp.int32, (tokens, tokens), 0)
        lanes = lax.broadcasted_iota(jnp.int32, (tokens, tokens), 1)
        spread = jnp.broadcast_to(fresh_frames[...], (tokens, tokens)).astype(jnp.float32)
        return jnp.sum(jnp.where(rows == lanes, spread, 0.0), axis=1, keepdims=True)

    def shown(frames, column):
        row = key_frames[frames].astype(jnp.float32)[None]
        return jnp.where(row <= column, 0.0, MASKED)

    def queries_of(hidden, head_gain):
        rows = []
        for g in range(GROUP):
            span = slice(g * HD, (g + 1) * HD)
            x = hidden[:, span]
            mean = jnp.mean(x * x, axis=1, keepdims=True)
            rows.append(x * lax.rsqrt(mean + EPSILON) * head_gain[:, span])
        return jnp.concatenate(rows, axis=0).astype(jnp.bfloat16)

    def attend(queries, head_keys, head_values, mask):
        scores = lax.dot_general(
            queries, head_keys, (((1,), (1,)), ((), ())), preferred_element_type=jnp.float32
        )
        block = 2 * tokens
        maxima, probs = [], []
        for g in range(head_rows // block):
            part = scores[g * block : (g + 1) * block] + mask
            top = jnp.max(part, axis=1, keepdims=True)
            maxima.append(top)
            probs.append(jnp.exp2((part - top) * EXPONENT_SCALE).astype(jnp.bfloat16))
        product = lax.dot_general(
            jnp.concatenate(probs, axis=0),
            head_values,
            (((1,), (0,)), ((), ())),
            preferred_element_type=jnp.float32,
        )
        return jnp.concatenate(maxima, axis=0), product

    def part_copy(tick, j):
        return remote(
            sent.at[tick, j],
            arrived.at[tick, chip],
            part_send_sem.at[tick, j],
            part_recv_sem.at[tick, chip],
            in_line(j),
        )

    def part_arrival(tick, j):
        return remote(
            sent.at[tick, j],
            arrived.at[tick, j],
            part_send_sem.at[tick, j],
            part_recv_sem.at[tick, j],
            in_line(j),
        )

    def ship(tick, step, top, totals, weighted):
        h = head_at(step)
        lanes = lax.broadcasted_iota(jnp.int32, (chunk_rows, HD), 1)
        pick = (
            lax.broadcasted_iota(jnp.int32, (STAT_ROWS, HD), 0)
            == lax.broadcasted_iota(jnp.int32, (STAT_ROWS, HD), 1)
        ).astype(jnp.bfloat16)
        packets = []
        for q in range(chunks_per_head):
            span = slice(q * chunk_rows, (q + 1) * chunk_rows)
            stats = jnp.where(lanes % 2 == 0, top[span], totals[span])
            high = stats.astype(jnp.bfloat16).astype(jnp.float32)
            middle = (stats - high).astype(jnp.bfloat16).astype(jnp.float32)
            low = stats - high - middle
            terms = jnp.where(lanes < 2, high, jnp.where(lanes < 4, middle, low))
            terms = lax.dot_general(
                pick, terms.astype(jnp.bfloat16), (((1,), (1,)), ((), ())),
                preferred_element_type=jnp.float32,
            )
            terms = jnp.concatenate(
                [terms, jnp.ones((STAT_ROWS, HD - chunk_rows), jnp.float32)], axis=1
            )
            packets.append(jnp.concatenate([weighted[span], terms], axis=0))
        if step:
            for q in range(chunks_per_head):
                j = h * chunks_per_head + q
                sent[tick, j] = packets[q].astype(jnp.bfloat16)
                part_copy(tick, j).start()
        else:
            even = chip % 2 == 0
            arrived[tick, chip] = jnp.where(even, packets[0], packets[1]).astype(jnp.bfloat16)
            j = chip + jnp.where(even, 1, -1)
            sent[tick, j] = jnp.where(even, packets[1], packets[0]).astype(jnp.bfloat16)
            part_copy(tick, j).start()

    def combine(tick, residual):
        @pl.loop(0, n_chips - 1)
        def _(k):
            part_arrival(tick, far_first(n_chips - 2 - k)).wait()

        stats = arrived[tick, :, chunk_rows:, :].astype(jnp.float32)
        tops = stats[:, 0] + stats[:, 2] + stats[:, 4]
        totals = stats[:, 1] + stats[:, 3] + stats[:, 5]
        overall = jnp.max(tops, axis=0, keepdims=True)
        factors = jnp.exp2((tops - overall) * EXPONENT_SCALE)
        factors = factors / jnp.sum(factors * totals, axis=0, keepdims=True)
        factors = jnp.concatenate(
            [factors, jnp.zeros((HD - n_chips, HD), jnp.float32)], axis=0
        ).T
        attended = jnp.zeros((chunk_rows, HD), jnp.float32)
        for j in range(n_chips):
            weighted = arrived[tick, j, :chunk_rows].astype(jnp.float32)
            attended += factors[:chunk_rows, j : j + 1] * weighted
        for g in range(heads_in_chunk):
            lanes = slice(g * HD, (g + 1) * HD)
            combined[tick, :, lanes] = (
                residual[:, lanes] + attended[g * tokens : (g + 1) * tokens]
            ).astype(jnp.bfloat16)

    mask = shown(own_frames, held_frames(section))
    bias[0:tokens, 0:own_keys] = mask
    bias[tokens : 2 * tokens, 0:own_keys] = mask
    pair_lanes = lax.broadcasted_iota(jnp.int32, (head_rows, HD), 1)

    def first_tick(own):
        for step in FARTHEST_FIRST:
            for copy in loads(own, step):
                copy.wait()
        for step in FARTHEST_FIRST:
            h = head_at(step)
            span = columns((core if own else other) * kv_heads + h, GROUP * HD)
            slot = slot_of(own, h)
            queries = queries_of(act[:, span].astype(jnp.float32), gain[:, span])
            top, product = attend(queries, keys[slot], values[slot], bias[:, 0:own_keys])
            place = own * kv_heads + h
            parts[place, :, :HD] = product[:, :HD]
            parts[place, :, HD:] = jnp.where(pair_lanes < HD // 2, top, product[:, HD:])

    first_tick(0)
    pl.semaphore_wait(barrier, n_chips + not_first.astype(jnp.int32) + not_last.astype(jnp.int32))

    def pair_copy(h):
        return remote(
            parts.at[h], pair_arrived.at[h], pair_send_sem.at[h], pair_recv_sem.at[h], sibling
        )

    for step in FARTHEST_FIRST:
        pair_copy(head_at(step)).start()

    frames_copy = remote(
        key_frames_hbm, key_frames.at[own_frames], frames_send_sem, frames_recv_sem, sibling
    )
    frames_copy.start()

    @pl.when(not_first)
    def _():
        pl.semaphore_signal(line_sem, inc=1, device_id=(section - 1, ctx), device_id_type=MESH)

    first_tick(1)

    for step in FARTHEST_FIRST:
        h = head_at(step)
        pair_copy(h).wait()
        own_top = parts[kv_heads + h, :, HD : HD + 1]
        own_totals = parts[kv_heads + h, :, 2 * HD - 1 :]
        pair_top = pair_arrived[h, :, HD : HD + 1]
        pair_totals = pair_arrived[h, :, 2 * HD - 1 :]
        top = jnp.maximum(own_top, pair_top)
        own_factor = jnp.exp2((own_top - top) * EXPONENT_SCALE)
        pair_factor = jnp.exp2((pair_top - top) * EXPONENT_SCALE)
        totals = own_factor * own_totals + pair_factor * pair_totals
        weighted = (
            own_factor * parts[kv_heads + h, :, :HD] + pair_factor * pair_arrived[h, :, :HD]
        )
        ship(0, step, top, totals, weighted)

    def cache_copies(h):
        from_slot, to_slot = 2 * kv_heads + h, 2 * h + core
        return (
            remote(
                keys.at[from_slot],
                keys.at[to_slot],
                cache_send_sem.at[h, 0],
                cache_recv_sem.at[h, 0],
                sibling,
            ),
            remote(
                values.at[from_slot, :, pl.ds(0, HD)],
                values.at[to_slot, :, pl.ds(0, HD)],
                cache_send_sem.at[h, 1],
                cache_recv_sem.at[h, 1],
                sibling,
            ),
        )

    def cache_arrivals(h):
        from_slot, to_slot = 2 * kv_heads + h, 2 * h + other
        return (
            remote(
                keys.at[from_slot],
                keys.at[to_slot],
                cache_send_sem.at[h, 0],
                cache_recv_sem.at[h, 0],
                sibling,
            ),
            remote(
                values.at[from_slot, :, pl.ds(0, HD)],
                values.at[to_slot, :, pl.ds(0, HD)],
                cache_send_sem.at[h, 1],
                cache_recv_sem.at[h, 1],
                sibling,
            ),
        )

    for copy in late:
        copy.wait()
    frames_copy.wait()
    column = jnp.where(not_first, held_frames(section - 1), entering_frames())
    for side in range(2):
        mask = shown(pl.ds(side * stride, own_keys), column)
        span = slice(side * own_keys, (side + 1) * own_keys)
        bias[0:tokens, span] = mask
        bias[tokens : 2 * tokens, span] = mask

    combine(0, act[:, columns(core * n_chips + chip, chunk_columns)].astype(jnp.float32))

    def hand_copy(j):
        return remote(
            combined.at[0],
            handed.at[:, columns(chip, chunk_columns)],
            hand_send_sem.at[j],
            hand_recv_sem.at[chip],
            (section + 1, j * 2 + core),
        )

    def hand_arrival(j):
        return remote(
            combined.at[0],
            handed.at[:, columns(j, chunk_columns)],
            hand_send_sem.at[j],
            hand_recv_sem.at[j],
            (section - 1, j * 2 + core),
        )

    @pl.when(not_last)
    def _():
        pl.semaphore_wait(line_sem, 1)

        @pl.loop(0, n_chips)
        def _(k):
            hand_copy(far_first(k)).start()

    for steps in SECOND_TICK_STEPS:
        for step in steps:
            for copy in cache_copies(head_at(step)):
                copy.start()

    def incoming(span):
        return jnp.where(
            not_first, handed[:, span].astype(jnp.float32), fresh[:, span].astype(jnp.float32)
        )

    for steps in SECOND_TICK_STEPS:
        for step in steps:
            for copy in cache_arrivals(head_at(step)):
                copy.wait()

        @pl.when(not_first)
        def _(steps=steps):
            for step in steps:
                for q in range(chunks_per_head):
                    hand_arrival(head_at(step) * chunks_per_head + q).wait_recv()

        results = []
        for step in steps:
            h = head_at(step)
            head_gain = gain[:, columns(core * kv_heads + h, GROUP * HD)]
            both = pl.ds(2 * h, 2)
            results.append(
                attend(
                    queries_of(incoming(columns(h, GROUP * HD)), head_gain),
                    keys[both].reshape(2 * own_keys, HD),
                    values[both].reshape(2 * own_keys, 2 * HD),
                    bias[...],
                )
            )
        for step, (top, product) in zip(steps, results):
            ship(1, step, top, product[:, HD:], product[:, :HD])

    combine(1, incoming(columns(chip, chunk_columns)))

    def result_columns(half, j):
        return columns(half * n_chips + j, chunk_columns)

    def out_copy(j):
        return remote(
            combined.at[1],
            out_ref.at[:, result_columns(core, chip)],
            out_send_sem.at[j],
            out_recv_sem.at[chip],
            in_line(j),
        )

    def out_arrival(j):
        return remote(
            combined.at[1],
            out_ref.at[:, result_columns(core, j)],
            out_send_sem.at[j],
            out_recv_sem.at[j],
            in_line(j),
        )

    def cross_copy(j, half):
        return remote(
            out_ref.at[:, result_columns(half, j)],
            out_ref.at[:, result_columns(half, j)],
            cross_send_sem.at[j],
            cross_recv_sem.at[j],
            sibling,
        )

    @pl.loop(0, n_chips - 1)
    def _(k):
        out_copy(far_first(k)).start()

    out_ref[:, result_columns(core, chip)] = combined[1]
    cross_copy(chip, core).start()

    @pl.loop(0, n_chips - 1)
    def _(k):
        j = far_first(n_chips - 2 - k)
        out_arrival(j).wait_recv()
        cross_copy(j, core).start()

    @pl.loop(0, n_chips)
    def _(j):
        @pl.when(not_last)
        def _():
            hand_copy(j).wait_send()

        @pl.when(j != chip)
        def _():
            out_copy(j).wait_send()

    @pl.loop(0, n_chips)
    def _(j):
        cross_copy(j, other).wait_recv()
        cross_copy(j, core).wait_send()


def attention(n_sections, n_chips, act, act_frames, fresh, fresh_frames, gain, keys, values, key_frames):
    tokens, width = act.shape
    own_keys = keys.shape[0]
    plane = width // 2
    kv_heads = plane // (GROUP * HD)
    chunk_columns = plane // n_chips
    packet_rows = chunk_columns // HD * tokens + STAT_ROWS
    dma = pltpu.SemaphoreType.DMA
    operands = [
        pltpu.with_memory_space_constraint(x, pltpu.HBM)
        for x in (act, act_frames, fresh, fresh_frames, gain, keys, values, key_frames)
    ]
    return pl.pallas_call(
        functools.partial(kernel, n_sections, n_chips),
        out_shape=jax.ShapeDtypeStruct((tokens, width), jnp.bfloat16),
        in_specs=[pl.BlockSpec(memory_space=pltpu.HBM)] * 8,
        out_specs=pl.BlockSpec(memory_space=pltpu.VMEM),
        scratch_shapes=[
            pltpu.VMEM((tokens, width), jnp.bfloat16),
            pltpu.VMEM((tokens, plane), jnp.bfloat16),
            pltpu.VMEM(act_frames.shape, jnp.int32),
            pltpu.VMEM(fresh_frames.shape, jnp.int32),
            pltpu.VMEM((1, width), jnp.float32),
            pltpu.VMEM((2 * frames_stride(own_keys),), jnp.int32),
            pltpu.VMEM((3 * kv_heads, own_keys, HD), jnp.bfloat16),
            pltpu.VMEM((3 * kv_heads, own_keys, 2 * HD), jnp.bfloat16),
            pltpu.VMEM((2 * tokens, 2 * own_keys), jnp.float32),
            pltpu.VMEM((2 * kv_heads, GROUP * tokens, 2 * HD), jnp.float32),
            pltpu.VMEM((kv_heads, GROUP * tokens, 2 * HD), jnp.float32),
            pltpu.VMEM((2, n_chips, packet_rows, HD), jnp.bfloat16),
            pltpu.VMEM((2, n_chips, packet_rows, HD), jnp.bfloat16),
            pltpu.VMEM((2, tokens, chunk_columns), jnp.bfloat16),
            pltpu.VMEM((tokens, plane), jnp.bfloat16),
            dma((6,)),
            dma((2 * kv_heads,)),
            dma((2 * kv_heads,)),
            dma((kv_heads,)),
            dma((kv_heads,)),
            dma((kv_heads, 2)),
            dma((kv_heads, 2)),
            dma,
            dma,
            dma((2, n_chips)),
            dma((2, n_chips)),
            dma((n_chips,)),
            dma((n_chips,)),
            dma((n_chips,)),
            dma((n_chips,)),
            dma((n_chips,)),
            dma((n_chips,)),
            pltpu.SemaphoreType.REGULAR,
        ],
        compiler_params=pltpu.CompilerParams(
            collective_id=0, has_side_effects=True, vmem_limit_bytes=48 * 2**20
        ),
        name="two_ticks",
    )(*operands)


def solution(mesh):
    n_sections, n_chips = mesh.shape["section"], mesh.shape["ctx"] // 2

    def body(act, act_frames, fresh, fresh_frames, gain, keys, values, key_frames):
        result = attention(
            n_sections,
            n_chips,
            act[0],
            act_frames.T,
            fresh,
            fresh_frames[None],
            gain,
            keys[0],
            values[0],
            key_frames,
        )
        return result[None]

    placed = (
        P("section", None, None),
        P(),
        P(),
        P(),
        P("section", None),
        P("section", "ctx", None),
        P("section", "ctx", None),
        P("ctx"),
    )
    return jax.shard_map(
        body, mesh=mesh, in_specs=placed, out_specs=P("section", None, None), check_vma=False
    )
```

```python
import functools
import math

import jax
import jax.numpy as jnp
from jax import lax
from jax.experimental import pallas as pl
from jax.experimental.pallas import tpu as pltpu
from jax.sharding import PartitionSpec as P

HD = 128
GROUP = 8
EPSILON = 1e-05
MASKED = -1e30
MESH = pl.DeviceIdType.MESH
EXPONENT_SCALE = HD**-0.5 * math.log2(math.e)
STAT_ROWS = 16
FARTHEST_FIRST = (2, 1, 3, 0)
SECOND_TICK_STEPS = ((2, 1), (3, 0))


def frames_stride(count):
    return -(-count // 1024) * 1024


def remote(src, dst, send_sem, recv_sem, device):
    return pltpu.make_async_remote_copy(
        src_ref=src,
        dst_ref=dst,
        send_sem=send_sem,
        recv_sem=recv_sem,
        device_id=device,
        device_id_type=MESH,
    )


def kernel(
    n_sections,
    n_chips,
    act_hbm,
    act_frames_hbm,
    fresh_hbm,
    fresh_frames_hbm,
    gain_hbm,
    keys_hbm,
    values_hbm,
    key_frames_hbm,
    out_ref,
    act,
    fresh,
    act_frames,
    fresh_frames,
    gain,
    key_frames,
    keys,
    values,
    bias,
    parts,
    pair_arrived,
    sent,
    arrived,
    combined,
    handed,
    local_sem,
    keys_sem,
    values_sem,
    pair_send_sem,
    pair_recv_sem,
    cache_send_sem,
    cache_recv_sem,
    frames_send_sem,
    frames_recv_sem,
    part_send_sem,
    part_recv_sem,
    hand_send_sem,
    hand_recv_sem,
    out_send_sem,
    out_recv_sem,
    cross_send_sem,
    cross_recv_sem,
    line_sem,
):
    tokens = act.shape[0]
    own_keys = keys_hbm.shape[0]
    plane = fresh.shape[1]
    kv_heads = plane // (GROUP * HD)
    head_rows = GROUP * tokens
    chunk_columns = plane // n_chips
    heads_in_chunk = chunk_columns // HD
    chunk_rows = heads_in_chunk * tokens
    chunks_per_head = head_rows // chunk_rows

    section = lax.axis_index("section")
    ctx = lax.axis_index("ctx")
    chip, core = ctx // 2, ctx % 2
    other = 1 - core
    sibling = (section, chip * 2 + other)
    not_first = section != 0
    not_last = section != n_sections - 1

    def in_line(j):
        return (section, j * 2 + core)

    def columns(j, width):
        return pl.ds(pl.multiple_of(j * width, width), width)

    def far_first(k):
        half = n_chips // 2
        step = jnp.where(k % 2 == 1, half - (k + 1) // 2, half + k // 2)
        return (chip + step) % n_chips

    def slot_of(own, h):
        return 2 * h + core if own else 2 * kv_heads + h

    def head_at(step):
        return (chip // chunks_per_head + step) % kv_heads

    def loads(own, step):
        h = head_at(step)
        span = columns((core if own else other) * kv_heads + h, HD)
        slot, i = slot_of(own, h), own * kv_heads + step
        return (
            pltpu.make_async_copy(keys_hbm.at[:, span], keys.at[slot], keys_sem.at[i]),
            pltpu.make_async_copy(
                values_hbm.at[:, span], values.at[slot, :, pl.ds(0, HD)], values_sem.at[i]
            ),
        )

    stride = frames_stride(own_keys)
    own_frames = pl.ds(pl.multiple_of(core * stride, stride), own_keys)
    small = [
        pltpu.make_async_copy(act_hbm, act, local_sem.at[0]),
        pltpu.make_async_copy(act_frames_hbm, act_frames, local_sem.at[1]),
        pltpu.make_async_copy(gain_hbm, gain, local_sem.at[2]),
        pltpu.make_async_copy(key_frames_hbm, key_frames.at[own_frames], local_sem.at[3]),
    ]
    late = [
        pltpu.make_async_copy(fresh_hbm.at[:, columns(core, plane)], fresh, local_sem.at[4]),
        pltpu.make_async_copy(fresh_frames_hbm, fresh_frames, local_sem.at[5]),
    ]
    for copy in small:
        copy.start()

    barrier = pltpu.get_barrier_semaphore()
    pl.semaphore_signal(barrier, inc=1, device_id=sibling, device_id_type=MESH)

    @pl.loop(0, n_chips - 1)
    def _(k):
        pl.semaphore_signal(barrier, inc=1, device_id=in_line(far_first(k)), device_id_type=MESH)

    @pl.when(not_first)
    def _():
        pl.semaphore_signal(barrier, inc=1, device_id=(section - 1, ctx), device_id_type=MESH)

    @pl.when(not_last)
    def _():
        pl.semaphore_signal(barrier, inc=1, device_id=(section + 1, ctx), device_id_type=MESH)

    for own in (0, 1):
        for step in FARTHEST_FIRST:
            for copy in loads(own, step):
                copy.start()
    for copy in late:
        copy.start()
    for slot in range(values.shape[0]):
        values[slot, :, HD:] = jnp.ones((own_keys, HD), values.dtype)
    for copy in small:
        copy.wait()

    def held_frames(s):
        lanes = lax.broadcasted_iota(jnp.int32, act_frames.shape, 1)
        spread = act_frames[...].astype(jnp.float32)
        return jnp.sum(jnp.where(lanes == s, spread, 0.0), axis=1, keepdims=True)

    def entering_frames():
        rows = lax.broadcasted_iota(jnp.int32, (tokens, tokens), 0)
        lanes = lax.broadcasted_iota(jnp.int32, (tokens, tokens), 1)
        spread = jnp.broadcast_to(fresh_frames[...], (tokens, tokens)).astype(jnp.float32)
        return jnp.sum(jnp.where(rows == lanes, spread, 0.0), axis=1, keepdims=True)

    def shown(frames, column):
        row = key_frames[frames].astype(jnp.float32)[None]
        return jnp.where(row <= column, 0.0, MASKED)

    def queries_of(hidden, head_gain):
        rows = []
        for g in range(GROUP):
            span = slice(g * HD, (g + 1) * HD)
            x = hidden[:, span]
            mean = jnp.mean(x * x, axis=1, keepdims=True)
            rows.append(x * lax.rsqrt(mean + EPSILON) * head_gain[:, span])
        return jnp.concatenate(rows, axis=0).astype(jnp.bfloat16)

    def attend(queries, head_keys, head_values, mask):
        scores = lax.dot_general(
            queries, head_keys, (((1,), (1,)), ((), ())), preferred_element_type=jnp.float32
        )
        block = 2 * tokens
        maxima, probs = [], []
        for g in range(head_rows // block):
            part = scores[g * block : (g + 1) * block] + mask
            top = jnp.max(part, axis=1, keepdims=True)
            maxima.append(top)
            probs.append(jnp.exp2((part - top) * EXPONENT_SCALE).astype(jnp.bfloat16))
        product = lax.dot_general(
            jnp.concatenate(probs, axis=0),
            head_values,
            (((1,), (0,)), ((), ())),
            preferred_element_type=jnp.float32,
        )
        return jnp.concatenate(maxima, axis=0), product

    def part_copy(tick, j):
        return remote(
            sent.at[tick, j],
            arrived.at[tick, chip],
            part_send_sem.at[tick, j],
            part_recv_sem.at[tick, chip],
            in_line(j),
        )

    def part_arrival(tick, j):
        return remote(
            sent.at[tick, j],
            arrived.at[tick, j],
            part_send_sem.at[tick, j],
            part_recv_sem.at[tick, j],
            in_line(j),
        )

    def ship(tick, step, top, totals, weighted):
        h = head_at(step)
        lanes = lax.broadcasted_iota(jnp.int32, (chunk_rows, HD), 1)
        packets = []
        for q in range(chunks_per_head):
            span = slice(q * chunk_rows, (q + 1) * chunk_rows)
            stats = jnp.where(lanes % 2 == 0, top[span], totals[span])
            high = stats.astype(jnp.bfloat16).astype(jnp.float32)
            middle = (stats - high).astype(jnp.bfloat16).astype(jnp.float32)
            low = stats - high - middle
            terms = jnp.where(lanes < 2, high, jnp.where(lanes < 4, middle, low))
            terms = jnp.concatenate(
                [terms, jnp.ones((HD - chunk_rows, HD), jnp.float32)], axis=0
            ).T[:STAT_ROWS]
            packets.append(jnp.concatenate([weighted[span], terms], axis=0))
        if step:
            for q in range(chunks_per_head):
                j = h * chunks_per_head + q
                sent[tick, j] = packets[q].astype(jnp.bfloat16)
                part_copy(tick, j).start()
        else:
            even = chip % 2 == 0
            arrived[tick, chip] = jnp.where(even, packets[0], packets[1]).astype(jnp.bfloat16)
            j = chip + jnp.where(even, 1, -1)
            sent[tick, j] = jnp.where(even, packets[1], packets[0]).astype(jnp.bfloat16)
            part_copy(tick, j).start()

    def combine(tick, residual):
        @pl.loop(0, n_chips - 1)
        def _(k):
            part_arrival(tick, far_first(n_chips - 2 - k)).wait()

        stats = arrived[tick, :, chunk_rows:, :].astype(jnp.float32)
        tops = stats[:, 0] + stats[:, 2] + stats[:, 4]
        totals = stats[:, 1] + stats[:, 3] + stats[:, 5]
        overall = jnp.max(tops, axis=0, keepdims=True)
        factors = jnp.exp2((tops - overall) * EXPONENT_SCALE)
        factors = factors / jnp.sum(factors * totals, axis=0, keepdims=True)
        factors = jnp.concatenate(
            [factors, jnp.zeros((HD - n_chips, HD), jnp.float32)], axis=0
        ).T
        attended = jnp.zeros((chunk_rows, HD), jnp.float32)
        for j in range(n_chips):
            weighted = arrived[tick, j, :chunk_rows].astype(jnp.float32)
            attended += factors[:chunk_rows, j : j + 1] * weighted
        for g in range(heads_in_chunk):
            lanes = slice(g * HD, (g + 1) * HD)
            combined[tick, :, lanes] = (
                residual[:, lanes] + attended[g * tokens : (g + 1) * tokens]
            ).astype(jnp.bfloat16)

    mask = shown(own_frames, held_frames(section))
    bias[0:tokens, 0:own_keys] = mask
    bias[tokens : 2 * tokens, 0:own_keys] = mask
    pair_lanes = lax.broadcasted_iota(jnp.int32, (head_rows, HD), 1)

    def first_tick(own):
        for step in FARTHEST_FIRST:
            for copy in loads(own, step):
                copy.wait()
        for step in FARTHEST_FIRST:
            h = head_at(step)
            span = columns((core if own else other) * kv_heads + h, GROUP * HD)
            slot = slot_of(own, h)
            queries = queries_of(act[:, span].astype(jnp.float32), gain[:, span])
            top, product = attend(queries, keys[slot], values[slot], bias[:, 0:own_keys])
            place = own * kv_heads + h
            parts[place, :, :HD] = product[:, :HD]
            parts[place, :, HD:] = jnp.where(pair_lanes < HD // 2, top, product[:, HD:])

    first_tick(0)
    pl.semaphore_wait(barrier, n_chips + not_first.astype(jnp.int32) + not_last.astype(jnp.int32))

    def pair_copy(h):
        return remote(
            parts.at[h], pair_arrived.at[h], pair_send_sem.at[h], pair_recv_sem.at[h], sibling
        )

    for step in FARTHEST_FIRST:
        pair_copy(head_at(step)).start()

    frames_copy = remote(
        key_frames_hbm, key_frames.at[own_frames], frames_send_sem, frames_recv_sem, sibling
    )
    frames_copy.start()

    @pl.when(not_first)
    def _():
        pl.semaphore_signal(line_sem, inc=1, device_id=(section - 1, ctx), device_id_type=MESH)

    first_tick(1)

    for step in FARTHEST_FIRST:
        h = head_at(step)
        pair_copy(h).wait()
        own_top = parts[kv_heads + h, :, HD : HD + 1]
        own_totals = parts[kv_heads + h, :, 2 * HD - 1 :]
        pair_top = pair_arrived[h, :, HD : HD + 1]
        pair_totals = pair_arrived[h, :, 2 * HD - 1 :]
        top = jnp.maximum(own_top, pair_top)
        own_factor = jnp.exp2((own_top - top) * EXPONENT_SCALE)
        pair_factor = jnp.exp2((pair_top - top) * EXPONENT_SCALE)
        totals = own_factor * own_totals + pair_factor * pair_totals
        weighted = (
            own_factor * parts[kv_heads + h, :, :HD] + pair_factor * pair_arrived[h, :, :HD]
        )
        ship(0, step, top, totals, weighted)

    def cache_copies(h):
        from_slot, to_slot = 2 * kv_heads + h, 2 * h + core
        return (
            remote(
                keys.at[from_slot],
                keys.at[to_slot],
                cache_send_sem.at[h, 0],
                cache_recv_sem.at[h, 0],
                sibling,
            ),
            remote(
                values.at[from_slot, :, pl.ds(0, HD)],
                values.at[to_slot, :, pl.ds(0, HD)],
                cache_send_sem.at[h, 1],
                cache_recv_sem.at[h, 1],
                sibling,
            ),
        )

    def cache_arrivals(h):
        from_slot, to_slot = 2 * kv_heads + h, 2 * h + other
        return (
            remote(
                keys.at[from_slot],
                keys.at[to_slot],
                cache_send_sem.at[h, 0],
                cache_recv_sem.at[h, 0],
                sibling,
            ),
            remote(
                values.at[from_slot, :, pl.ds(0, HD)],
                values.at[to_slot, :, pl.ds(0, HD)],
                cache_send_sem.at[h, 1],
                cache_recv_sem.at[h, 1],
                sibling,
            ),
        )

    for copy in late:
        copy.wait()
    frames_copy.wait()
    column = jnp.where(not_first, held_frames(section - 1), entering_frames())
    for side in range(2):
        mask = shown(pl.ds(side * stride, own_keys), column)
        span = slice(side * own_keys, (side + 1) * own_keys)
        bias[0:tokens, span] = mask
        bias[tokens : 2 * tokens, span] = mask

    combine(0, act[:, columns(core * n_chips + chip, chunk_columns)].astype(jnp.float32))

    def hand_copy(j):
        return remote(
            combined.at[0],
            handed.at[:, columns(chip, chunk_columns)],
            hand_send_sem.at[j],
            hand_recv_sem.at[chip],
            (section + 1, j * 2 + core),
        )

    def hand_arrival(j):
        return remote(
            combined.at[0],
            handed.at[:, columns(j, chunk_columns)],
            hand_send_sem.at[j],
            hand_recv_sem.at[j],
            (section - 1, j * 2 + core),
        )

    @pl.when(not_last)
    def _():
        pl.semaphore_wait(line_sem, 1)

        @pl.loop(0, n_chips)
        def _(k):
            hand_copy(far_first(k)).start()

    for steps in SECOND_TICK_STEPS:
        for step in steps:
            for copy in cache_copies(head_at(step)):
                copy.start()

    def incoming(span):
        return jnp.where(
            not_first, handed[:, span].astype(jnp.float32), fresh[:, span].astype(jnp.float32)
        )

    for steps in SECOND_TICK_STEPS:
        for step in steps:
            for copy in cache_arrivals(head_at(step)):
                copy.wait()

        @pl.when(not_first)
        def _(steps=steps):
            for step in steps:
                for q in range(chunks_per_head):
                    hand_arrival(head_at(step) * chunks_per_head + q).wait_recv()

        results = []
        for step in steps:
            h = head_at(step)
            head_gain = gain[:, columns(core * kv_heads + h, GROUP * HD)]
            both = pl.ds(2 * h, 2)
            results.append(
                attend(
                    queries_of(incoming(columns(h, GROUP * HD)), head_gain),
                    keys[both].reshape(2 * own_keys, HD),
                    values[both].reshape(2 * own_keys, 2 * HD),
                    bias[...],
                )
            )
        for step, (top, product) in zip(steps, results):
            ship(1, step, top, product[:, HD:], product[:, :HD])

    combine(1, incoming(columns(chip, chunk_columns)))

    def result_columns(half, j):
        return columns(half * n_chips + j, chunk_columns)

    def out_copy(j):
        return remote(
            combined.at[1],
            out_ref.at[:, result_columns(core, chip)],
            out_send_sem.at[j],
            out_recv_sem.at[chip],
            in_line(j),
        )

    def out_arrival(j):
        return remote(
            combined.at[1],
            out_ref.at[:, result_columns(core, j)],
            out_send_sem.at[j],
            out_recv_sem.at[j],
            in_line(j),
        )

    def cross_copy(j, half):
        return remote(
            out_ref.at[:, result_columns(half, j)],
            out_ref.at[:, result_columns(half, j)],
            cross_send_sem.at[j],
            cross_recv_sem.at[j],
            sibling,
        )

    @pl.loop(0, n_chips - 1)
    def _(k):
        out_copy(far_first(k)).start()

    out_ref[:, result_columns(core, chip)] = combined[1]
    cross_copy(chip, core).start()

    @pl.loop(0, n_chips - 1)
    def _(k):
        j = far_first(n_chips - 2 - k)
        out_arrival(j).wait_recv()
        cross_copy(j, core).start()

    @pl.loop(0, n_chips)
    def _(j):
        @pl.when(not_last)
        def _():
            hand_copy(j).wait_send()

        @pl.when(j != chip)
        def _():
            out_copy(j).wait_send()

    @pl.loop(0, n_chips)
    def _(j):
        cross_copy(j, other).wait_recv()
        cross_copy(j, core).wait_send()


def attention(n_sections, n_chips, act, act_frames, fresh, fresh_frames, gain, keys, values, key_frames):
    tokens, width = act.shape
    own_keys = keys.shape[0]
    plane = width // 2
    kv_heads = plane // (GROUP * HD)
    chunk_columns = plane // n_chips
    packet_rows = chunk_columns // HD * tokens + STAT_ROWS
    dma = pltpu.SemaphoreType.DMA
    operands = [
        pltpu.with_memory_space_constraint(x, pltpu.HBM)
        for x in (act, act_frames, fresh, fresh_frames, gain, keys, values, key_frames)
    ]
    return pl.pallas_call(
        functools.partial(kernel, n_sections, n_chips),
        out_shape=jax.ShapeDtypeStruct((tokens, width), jnp.bfloat16),
        in_specs=[pl.BlockSpec(memory_space=pltpu.HBM)] * 8,
        out_specs=pl.BlockSpec(memory_space=pltpu.VMEM),
        scratch_shapes=[
            pltpu.VMEM((tokens, width), jnp.bfloat16),
            pltpu.VMEM((tokens, plane), jnp.bfloat16),
            pltpu.VMEM(act_frames.shape, jnp.int32),
            pltpu.VMEM(fresh_frames.shape, jnp.int32),
            pltpu.VMEM((1, width), jnp.float32),
            pltpu.VMEM((2 * frames_stride(own_keys),), jnp.int32),
            pltpu.VMEM((3 * kv_heads, own_keys, HD), jnp.bfloat16),
            pltpu.VMEM((3 * kv_heads, own_keys, 2 * HD), jnp.bfloat16),
            pltpu.VMEM((2 * tokens, 2 * own_keys), jnp.float32),
            pltpu.VMEM((2 * kv_heads, GROUP * tokens, 2 * HD), jnp.float32),
            pltpu.VMEM((kv_heads, GROUP * tokens, 2 * HD), jnp.float32),
            pltpu.VMEM((2, n_chips, packet_rows, HD), jnp.bfloat16),
            pltpu.VMEM((2, n_chips, packet_rows, HD), jnp.bfloat16),
            pltpu.VMEM((2, tokens, chunk_columns), jnp.bfloat16),
            pltpu.VMEM((tokens, plane), jnp.bfloat16),
            dma((6,)),
            dma((2 * kv_heads,)),
            dma((2 * kv_heads,)),
            dma((kv_heads,)),
            dma((kv_heads,)),
            dma((kv_heads, 2)),
            dma((kv_heads, 2)),
            dma,
            dma,
            dma((2, n_chips)),
            dma((2, n_chips)),
            dma((n_chips,)),
            dma((n_chips,)),
            dma((n_chips,)),
            dma((n_chips,)),
            dma((n_chips,)),
            dma((n_chips,)),
            pltpu.SemaphoreType.REGULAR,
        ],
        compiler_params=pltpu.CompilerParams(
            collective_id=0, has_side_effects=True, vmem_limit_bytes=48 * 2**20
        ),
        name="two_ticks",
    )(*operands)


def solution(mesh):
    n_sections, n_chips = mesh.shape["section"], mesh.shape["ctx"] // 2

    def body(act, act_frames, fresh, fresh_frames, gain, keys, values, key_frames):
        result = attention(
            n_sections,
            n_chips,
            act[0],
            act_frames.T,
            fresh,
            fresh_frames[None],
            gain,
            keys[0],
            values[0],
            key_frames,
        )
        return result[None]

    placed = (
        P("section", None, None),
        P(),
        P(),
        P(),
        P("section", None),
        P("section", "ctx", None),
        P("section", "ctx", None),
        P("ctx"),
    )
    return jax.shard_map(
        body, mesh=mesh, in_specs=placed, out_specs=P("section", None, None), check_vma=False
    )
```
